512 devices in a mesh: tile: 64 (over y, z_hi, core), layer: 8 (over x, z_lo).
Axes of the slice: x: 4, y: 8, z: 8 (z_hi: 4, z_lo: 2; z = z_hi * 2 + z_lo), core: 2. Of those that a mesh axis runs over, the one named last changes fastest.
Arguments:
- class_index: int32 [8, 2, 1024, 8192], P('layer', None, 'tile'), may hold values from 0 to 15
- class_conductance: float32 [8, 16], P('layer'), may hold values from 0.5 to 8
- loads: float32 [8, 1024, 8192], P('layer', 'tile'), may hold values from -4 to 4
- start_volts: float32 [8, 1024, 8192], P('layer', 'tile'), may hold values from 0.8 to 1
- via_cells: int32 [8, 524288], P('layer', 'tile'), may hold values from 0 to 15, as said below
- via_counts: int32 [8, 524288], P('layer', 'tile'), may hold values from 0 to 4
Outputs:
- volts: float32 [8, 1024, 8192], P('layer', 'tile')
The draws below stay inside these ranges and needn't reach their ends.
Inputs may be any that keep to these rules, and one draw needn't show every extreme that they name: `via_cells`: each slot names a row of its own strip; slot s sits in column s % 8192, so each column of a strip holds exactly one slot of each layer.
All inputs are finite; a program needn't handle non-finite values.
Results may differ from the reference program's by a relative error of at most 0.00002.
Values sent between devices are 32-bit elements; how exact they have to be, the bound alone decides.
A program may use at most 64 MiB of HBM per device.

```python
import math
import jax
import jax.numpy as jnp

ROWS = 16
COLS = 8192
CLASSES = 16
OUTER = 2
SWEEPS = 3
VIAS_DEV = 8192
LAYERS = 8
TILES = 64


def draw_via_cells(key, part):
    values = jax.random.randint(key, (LAYERS, TILES * VIAS_DEV), 0, ROWS, dtype=jnp.int32)
    values = values.at[0, 0].set(ROWS - 1)
    values = values.at[0, 1].set(0)
    return values


def plant(drawn, stream_key, smallest, high):
    place = [jax.random.randint(jax.random.fold_in(stream_key, axis), (), 0, length) for axis, length in enumerate(drawn.shape)]
    longest = drawn.shape.index(max(drawn.shape))
    neighbour = place[:longest] + [(place[longest] + 1) % drawn.shape[longest]] + place[longest + 1:]
    return drawn.at[tuple(place)].set(smallest).at[tuple(neighbour)].set(high)


def levels(own_key, shape, cuts, low, high):
    gain, own = 1.0, jax.random.fold_in(own_key, 6)
    for dim, shards_of in cuts:
        steps = jnp.exp(jax.random.uniform(jax.random.fold_in(own, dim), (shards_of,), jnp.float32, low / len(cuts), high / len(cuts)))
        gain = gain * jnp.repeat(steps, shape[dim] // shards_of).reshape([-1 if axis == dim else 1 for axis in range(len(shape))])
    return gain


def centred(key, shape, spread, most, split=(), kind=jnp.bfloat16):
    array = jax.random.normal(key, shape, jnp.float32) * spread
    if len(split) > 0:
        array = levels(key, shape, split, -0.22, 0.18) * array
    return jnp.clip(array, min=-most, max=most).astype(kind)


def setup_inputs(seed: int = 0) -> dict:
    keys = jax.random.split(jax.random.key(seed), 7)
    return {
        "class_index": plant(jax.random.randint(keys[0], (LAYERS, 2, ROWS * TILES, COLS), 0, CLASSES), jax.random.fold_in(keys[0], 1), 0, CLASSES - 1).astype(jnp.int32),
        "class_conductance": jnp.clip(jnp.exp(math.log(8.0) - 2.7725887 * jax.random.uniform(keys[1], (LAYERS, CLASSES), jnp.float32) ** levels(keys[1], (LAYERS, CLASSES), ((0, 8),), -0.2, 0.2)), 0.5, 8.0),
        "loads": centred(keys[2], (LAYERS, ROWS * TILES, COLS), 0.3, 4.0, ((0, 8), (1, 64)), jnp.float32),
        "start_volts": jnp.clip(0.8 + 0.19999999 * jax.random.uniform(keys[3], (LAYERS, ROWS * TILES, COLS), jnp.float32) ** levels(keys[3], (LAYERS, ROWS * TILES, COLS), ((0, 8), (1, 64)), -0.2, 0.2), 0.8, 1.0),
        "via_cells": draw_via_cells(jax.random.fold_in(keys[6], 71), 0),
        "via_counts": plant(jax.random.randint(keys[5], (LAYERS, TILES * VIAS_DEV), 0, 5), jax.random.fold_in(keys[5], 1), 0, 4).astype(jnp.int32),
    }


VIA_UNIT = 2.0
LOWER_BOUND = 0.05
UPPER_BOUND = 2.0


def chebyshev_terms(count):
    centre_value = 0.5 * (UPPER_BOUND + LOWER_BOUND)
    half_width = 0.5 * (UPPER_BOUND - LOWER_BOUND)
    sigma = centre_value / half_width
    rho_last = 1.0 / sigma
    terms = [(0.0, 1.0 / centre_value)]
    for index in range(1, count):
        rho_next = 1.0 / (2.0 * sigma - rho_last)
        terms.append((rho_next * rho_last, 2.0 * rho_next / half_width))
        rho_last = rho_next
    return terms


def lookup(class_codes, class_table):
    result = jnp.zeros(class_codes.shape, jnp.float32)
    for code in range(CLASSES):
        result = result + jnp.where(class_codes == code, class_table[code], jnp.float32(0.0))
    return result


def neighbours(padded, vertical_links, across):
    span = padded.shape[0]
    centre_cells = padded[1:span - 1]
    vertical = vertical_links[0:span - 2] * padded[0:span - 2] + vertical_links[1:span - 1] * padded[2:span]
    right_flow = jnp.pad(centre_cells[:, 1:], ((0, 0), (0, 1))) * across
    left_flow = jnp.pad(centre_cells[:, :-1] * across[:, :-1], ((0, 0), (1, 0)))
    return vertical + right_flow + left_flow


def relax_sweep(padded, vertical_links, across, right_side, inverse_diag, previous, factors):
    centre_cells = padded[1:-1]
    residual = inverse_diag * (right_side + neighbours(padded, vertical_links, across)) - centre_cells
    if previous is None:
        update = factors[1] * residual
    else:
        update = factors[0] * previous + factors[1] * residual
    return centre_cells + update, update


def reference(class_index, class_conductance, loads, start_volts, via_cells, via_counts):
    row_total = ROWS * TILES
    cell_total = row_total * COLS
    slots = jnp.arange(TILES * VIAS_DEV, dtype=jnp.int32)
    strip_row = (slots // VIAS_DEV) * ROWS
    slot_col = slots % COLS
    weights = VIA_UNIT * via_counts.astype(jnp.float32)
    factors = chebyshev_terms(SWEEPS)
    col_ids = jax.lax.broadcasted_iota(jnp.int32, (row_total, COLS), 1)
    row_ids = jax.lax.broadcasted_iota(jnp.int32, (row_total, COLS), 0)
    global_cells = [(strip_row + via_cells[layer_index]) * COLS + slot_col for layer_index in range(LAYERS)]
    across_all, links_all, inverse_all = [], [], []
    for layer_index in range(LAYERS):
        conductance = lookup(class_index[layer_index], class_conductance[layer_index])
        across = jnp.where(col_ids < COLS - 1, conductance[0], jnp.float32(0.0))
        downward = jnp.where(row_ids < row_total - 1, conductance[1], jnp.float32(0.0))
        vertical_links = jnp.concatenate([jnp.zeros((1, COLS), jnp.float32), downward], axis=0)
        via_diag = jnp.zeros((cell_total,), jnp.float32).at[global_cells[layer_index]].add(weights[layer_index])
        if layer_index > 0:
            via_diag = via_diag.at[global_cells[layer_index - 1]].add(weights[layer_index - 1])
        diagonal = across + jnp.pad(across[:, :-1], ((0, 0), (1, 0))) + vertical_links[:-1] + vertical_links[1:] + via_diag.reshape(row_total, COLS)
        across_all.append(across)
        links_all.append(vertical_links)
        inverse_all.append(1.0 / diagonal)
    volts = [start_volts[layer_index] for layer_index in range(LAYERS)]
    for outer_index in range(OUTER):
        renewed = []
        for layer_index in range(LAYERS):
            if layer_index < LAYERS - 1:
                above = volts[layer_index + 1].reshape(-1)[global_cells[layer_index]]
            else:
                above = jnp.ones((TILES * VIAS_DEV,), jnp.float32)
            source = jnp.zeros((cell_total,), jnp.float32).at[global_cells[layer_index]].add(weights[layer_index] * above)
            if layer_index > 0:
                below = volts[layer_index - 1].reshape(-1)[global_cells[layer_index - 1]]
                source = source.at[global_cells[layer_index - 1]].add(weights[layer_index - 1] * below)
            right_side = source.reshape(row_total, COLS) - loads[layer_index]
            current = volts[layer_index]
            update = None
            for sweep_index in range(SWEEPS):
                padded = jnp.pad(current, ((1, 1), (0, 0)))
                current, update = relax_sweep(padded, links_all[layer_index], across_all[layer_index], right_side, inverse_all[layer_index], update, factors[sweep_index])
            renewed.append(current)
        volts = renewed
    return jnp.stack(volts)
```

```python
import functools

import jax
import jax.numpy as jnp
from jax import lax
from jax.experimental import pallas as pl
from jax.experimental.pallas import tpu as pltpu
from jax.sharding import PartitionSpec as P

CLASSES = 16
OUTER = 2
SWEEPS = 3
VIA_UNIT = 2.0
LOWER_BOUND = 0.05
UPPER_BOUND = 2.0
LANES = 128
SUB = 8
MESH = pl.DeviceIdType.MESH


def chebyshev_terms(count):
    centre_value = 0.5 * (UPPER_BOUND + LOWER_BOUND)
    half_width = 0.5 * (UPPER_BOUND - LOWER_BOUND)
    sigma = centre_value / half_width
    rho_last = 1.0 / sigma
    terms = [(0.0, 1.0 / centre_value)]
    for index in range(1, count):
        rho_next = 1.0 / (2.0 * sigma - rho_last)
        terms.append((rho_next * rho_last, 2.0 * rho_next / half_width))
        rho_last = rho_next
    return terms


def kernel(
    rows,
    blocks,
    table,
    class_hbm,
    loads_hbm,
    volts_hbm,
    cells_hbm,
    counts_hbm,
    out_hbm,
    x,
    cls,
    to_right,
    to_left,
    to_up,
    to_down,
    drawn,
    right_side,
    links_in,
    halo,
    own_cells,
    own_counts,
    low_cells,
    low_counts,
    picked,
    below,
    above,
    scale,
    flow,
    in_sem,
    class_sem,
    via_sem,
    out_sem,
    send_sem,
    recv_sem,
):
    tile = lax.axis_index("tile")
    layer = lax.axis_index("layer")
    tiles = lax.axis_size("tile")
    layers = lax.axis_size("layer")
    next_tile = {"tile": lax.rem(tile + 1, tiles)}
    prev_tile = {"tile": lax.rem(tile + tiles - 1, tiles)}
    next_layer = {"layer": lax.rem(layer + 1, layers)}
    prev_layer = {"layer": lax.rem(layer + layers - 1, layers)}
    last = rows - 1
    sweeps = OUTER * SWEEPS

    cells_in = pltpu.make_async_copy(cells_hbm, own_cells, via_sem.at[0])
    counts_in = pltpu.make_async_copy(counts_hbm, own_counts, via_sem.at[1])
    cells_in.start()

    def load_volts(r, _):
        pltpu.make_async_copy(
            volts_hbm.at[r // SUB, :, lax.rem(r, SUB)], x.at[0, r], in_sem.at[0]
        ).start()
        return 0

    def load_links(r, _):
        for k in range(2):
            pltpu.make_async_copy(
                class_hbm.at[k, r // SUB, :, lax.rem(r, SUB)], cls.at[k, r], class_sem.at[0]
            ).start()
        return 0

    def load_loads(r, _):
        pltpu.make_async_copy(
            loads_hbm.at[r // SUB, :, lax.rem(r, SUB)], drawn.at[r], in_sem.at[1]
        ).start()
        return 0

    lax.fori_loop(0, rows, load_volts, 0)
    counts_in.start()
    lax.fori_loop(0, rows, load_links, 0)
    lax.fori_loop(0, rows, load_loads, 0)

    barrier = pltpu.get_barrier_semaphore()
    for peer in (next_tile, prev_tile, next_layer, prev_layer):
        pl.semaphore_signal(barrier, inc=1, device_id=peer, device_id_type=MESH)

    sent = []

    def remote(src, dst, peer):
        slot = len(sent)
        copy = pltpu.make_async_remote_copy(
            src_ref=src,
            dst_ref=dst,
            send_sem=send_sem.at[slot],
            recv_sem=recv_sem.at[slot],
            device_id=peer,
            device_id_type=MESH,
        )
        copy.start()
        sent.append(copy)
        return copy

    def exchange(step):
        upper = remote(x.at[step, last], halo.at[step, 0], next_tile)
        lower = remote(x.at[step, 0], halo.at[step, 1], prev_tile)
        return upper, lower

    lane = lax.broadcasted_iota(jnp.int32, (blocks, LANES), 1)
    zero = jnp.float32(0.0)

    def pick(step, cells):
        def body(r, acc):
            return jnp.where(cells == r, x[step, r], acc)

        return lax.fori_loop(0, rows, body, jnp.zeros((blocks, LANES), jnp.float32), unroll=True)

    cells_in.wait()
    counts_in.wait()
    pl.semaphore_wait(barrier, 4)
    cells_up = remote(own_cells, low_cells, next_layer)
    pltpu.make_async_copy(x.at[1], x.at[0], in_sem.at[0]).wait()
    picked[0] = pick(0, own_cells[...])
    volts_up = remote(picked.at[0], below.at[0], next_layer)
    halos = exchange(0)
    counts_up = remote(own_counts, low_counts, next_layer)

    pltpu.make_async_copy(cls, cls, class_sem.at[0]).wait()
    table_lane = lax.broadcasted_iota(jnp.int32, (SUB, LANES), 1)
    values = jnp.zeros((SUB, LANES), jnp.float32)
    for code in range(CLASSES):
        values = jnp.where(table_lane == code, table[0, code], values)

    def look_up(codes):
        return jnp.concatenate(
            [
                jnp.take_along_axis(
                    values, codes[SUB * k : SUB * (k + 1)], axis=1, mode="promise_in_bounds"
                )
                for k in range(blocks // SUB)
            ],
            axis=0,
        )

    to_down[last] = jnp.where(tile == tiles - 1, zero, look_up(cls[1, last]))
    links_down = remote(to_down.at[last], links_in, next_tile)

    block_ids = lax.broadcasted_iota(jnp.int32, (blocks, LANES), 0)
    at_end = jnp.logical_and(block_ids == blocks - 1, lane == LANES - 1)

    def look_up_row(r, _):
        to_right[r] = jnp.where(at_end, zero, look_up(cls[0, r]))

        @pl.when(r < last)
        def _():
            to_down[r] = look_up(cls[1, r])

        return 0

    lax.fori_loop(0, rows, look_up_row, 0)

    cells_up.wait_recv()
    picked[1] = pick(0, low_cells[...])
    volts_down = remote(picked.at[1], above.at[0], prev_layer)

    counts_up.wait_recv()
    links_down.wait_recv()
    pltpu.make_async_copy(drawn, drawn, in_sem.at[1]).wait()

    def right_of(v):
        turned = pltpu.roll(v, LANES - 1, 1)
        return jnp.where(lane == LANES - 1, pltpu.roll(turned, blocks - 1, 0), turned)

    def left_of(v):
        turned = pltpu.roll(v, 1, 1)
        return jnp.where(lane == 0, pltpu.roll(turned, 1, 0), turned)

    scale[0] = VIA_UNIT * own_counts[...].astype(jnp.float32)
    scale[1] = jnp.where(layer == 0, zero, VIA_UNIT * low_counts[...].astype(jnp.float32))
    scale[2] = jnp.zeros((blocks, LANES), jnp.float32)
    scale[3] = jnp.zeros((blocks, LANES), jnp.float32)
    sent_links = []

    def coefficients(r, up, down):
        own = own_cells[...] == r
        low = low_cells[...] == r
        across = to_right[r]
        before = left_of(across)
        diagonal = (
            across + before + up + down + jnp.where(own, scale[0], zero) + jnp.where(low, scale[1], zero)
        )
        inverse = 1.0 / diagonal
        to_right[r] = inverse * across
        to_left[r] = inverse * before
        to_up[r] = inverse * up
        drawn[r] = inverse * drawn[r]
        scale[2] = jnp.where(own, inverse, scale[2])
        scale[3] = jnp.where(low, inverse, scale[3])
        return inverse * down

    def coefficients_row(r, _):
        flow[r] = coefficients(r, to_down[r - 1], to_down[r])
        return 0

    flow[0] = coefficients(0, links_in[...], to_down[0])
    lax.fori_loop(1, rows, coefficients_row, 0)
    scale[2] = scale[2] * scale[0]
    scale[3] = scale[3] * scale[1]

    def sweep_row(step, r, upper, lower, first_of_step):
        here = x[step, r]
        if first_of_step:
            side = (
                jnp.where(own_cells[...] == r, scale[0], zero)
                + jnp.where(low_cells[...] == r, scale[1], zero)
                - drawn[r]
            )
            right_side[r] = side
        else:
            side = right_side[r]
        fore, aft = factors[step % SWEEPS]
        total = (
            side
            + to_right[r] * right_of(here)
            + to_left[r] * left_of(here)
            + to_up[r] * upper
            + flow[r] * lower
        )
        update = jnp.float32(aft) * (total - here)
        if step % SWEEPS:
            update = update + jnp.float32(fore) * (here - x[step - 1, r])
        x[step + 1, r] = here + update

    factors = chebyshev_terms(SWEEPS)
    waits = None
    out_copies = []
    for step in range(sweeps):
        first = step % SWEEPS == 0
        if first:
            volts_up.wait_recv()
            volts_down.wait_recv()
            outer = step // SWEEPS
            top = jnp.where(layer == layers - 1, jnp.float32(1.0), above[outer])
            scale[0] = scale[2] * top
            scale[1] = scale[3] * below[outer]

        def inner_row(r, _, step=step, first=first):
            sweep_row(step, r, x[step, r - 1], x[step, r + 1], first)
            if step == sweeps - 1:
                pltpu.make_async_copy(
                    x.at[sweeps, r], out_hbm.at[r // SUB, :, lax.rem(r, SUB)], out_sem
                ).start()
            return 0

        lax.fori_loop(1, last, inner_row, 0)
        halos[0].wait_recv()
        sweep_row(step, 0, halo[step, 0], x[step, 1], first)
        halos[1].wait_recv()
        sweep_row(step, last, x[step, last - 1], halo[step, 1], first)
        if step < sweeps - 1:
            halos = exchange(step + 1)
        if step + 1 < sweeps and (step + 1) % SWEEPS == 0:
            outer = (step + 1) // SWEEPS
            picked[2 * outer] = pick(step + 1, own_cells[...])
            volts_up = remote(picked.at[2 * outer], below.at[outer], next_layer)
            picked[2 * outer + 1] = pick(step + 1, low_cells[...])
            volts_down = remote(picked.at[2 * outer + 1], above.at[outer], prev_layer)
    for r in (0, last):
        pltpu.make_async_copy(x.at[sweeps, r], out_hbm.at[r // SUB, :, r % SUB], out_sem).start()
    pltpu.make_async_copy(x.at[sweeps], x.at[sweeps], out_sem).wait()
    for copy in sent:
        copy.wait_send()


def local(class_index, class_conductance, loads, start_volts, via_cells, via_counts):
    rows, cols = loads.shape[1:]
    blocks = cols // LANES
    groups = rows // SUB

    def folded(a):
        lead = a.shape[:-2]
        a = a.reshape(*lead, groups, SUB, blocks, LANES)
        return jnp.swapaxes(a, -3, -2)

    classes = folded(class_index[0])
    drawn = folded(loads[0])
    volts = folded(start_volts[0])
    cells = via_cells.reshape(blocks, LANES)
    counts = via_counts.reshape(blocks, LANES)
    grid = (rows, blocks, LANES)
    row = (blocks, LANES)
    f32, i32 = jnp.float32, jnp.int32
    copies = 2 * OUTER * SWEEPS + 1 + 2 + 2 * OUTER
    vmem = pltpu.VMEM


    out = pl.pallas_call(
        functools.partial(kernel, rows, blocks),
        out_shape=jax.ShapeDtypeStruct((groups, blocks, SUB, LANES), f32),
        in_specs=[pl.BlockSpec(memory_space=pltpu.SMEM)] + [pl.BlockSpec(memory_space=pl.ANY)] * 5,
        out_specs=pl.BlockSpec(memory_space=pl.ANY),
        scratch_shapes=[
            vmem((OUTER * SWEEPS + 1, *grid), f32),
            vmem((2, *grid), i32),
            vmem(grid, f32),
            vmem(grid, f32),
            vmem(grid, f32),
            vmem(grid, f32),
            vmem(grid, f32),
            vmem(grid, f32),
            vmem(row, f32),
            vmem((OUTER * SWEEPS, 2, *row), f32),
            vmem(row, i32),
            vmem(row, i32),
            vmem(row, i32),
            vmem(row, i32),
            vmem((2 * OUTER, *row), f32),
            vmem((OUTER, *row), f32),
            vmem((OUTER, *row), f32),
            vmem((4, *row), f32),
            vmem(grid, f32),
            pltpu.SemaphoreType.DMA((2,)),
            pltpu.SemaphoreType.DMA((1,)),
            pltpu.SemaphoreType.DMA((2,)),
            pltpu.SemaphoreType.DMA,
            pltpu.SemaphoreType.DMA((copies,)),
            pltpu.SemaphoreType.DMA((copies,)),
        ],
        compiler_params=pltpu.CompilerParams(
            collective_id=0, has_side_effects=True, vmem_limit_bytes=60 * 1024 * 1024
        ),
    )(class_conductance, classes, drawn, volts, cells, counts)
    return jnp.swapaxes(out, 1, 2).reshape(1, rows, cols)


def solution(mesh):
    placed = (
        P("layer", None, "tile", None),
        P("layer", None),
        P("layer", "tile", None),
        P("layer", "tile", None),
        P("layer", "tile"),
        P("layer", "tile"),
    )
    return jax.shard_map(
        local, mesh=mesh, in_specs=placed, out_specs=P("layer", "tile", None), check_vma=False
    )
```

```python
import functools

import jax
import jax.numpy as jnp
from jax import lax
from jax.experimental import pallas as pl
from jax.experimental.pallas import tpu as pltpu
from jax.sharding import PartitionSpec as P

CLASSES = 16
OUTER = 2
SWEEPS = 3
VIA_UNIT = 2.0
LOWER_BOUND = 0.05
UPPER_BOUND = 2.0
LANES = 128
SUB = 8
MESH = pl.DeviceIdType.MESH


def chebyshev_terms(count):
    centre_value = 0.5 * (UPPER_BOUND + LOWER_BOUND)
    half_width = 0.5 * (UPPER_BOUND - LOWER_BOUND)
    sigma = centre_value / half_width
    rho_last = 1.0 / sigma
    terms = [(0.0, 1.0 / centre_value)]
    for index in range(1, count):
        rho_next = 1.0 / (2.0 * sigma - rho_last)
        terms.append((rho_next * rho_last, 2.0 * rho_next / half_width))
        rho_last = rho_next
    return terms


def kernel(
    rows,
    blocks,
    table,
    class_hbm,
    loads_hbm,
    volts_hbm,
    cells_hbm,
    counts_hbm,
    out_hbm,
    x,
    cls,
    links,
    drawn,
    right_side,
    down_links,
    links_in,
    ghost_links,
    halo,
    halo_pair,
    halo_side,
    ghost,
    own_cells,
    own_counts,
    low_cells,
    low_counts,
    picked,
    below,
    above,
    scale,
    in_sem,
    class_sem,
    via_sem,
    out_sem,
    send_sem,
    recv_sem,
):
    tile = lax.axis_index("tile")
    layer = lax.axis_index("layer")
    tiles = lax.axis_size("tile")
    layers = lax.axis_size("layer")
    next_tile = {"tile": lax.rem(tile + 1, tiles)}
    prev_tile = {"tile": lax.rem(tile + tiles - 1, tiles)}
    next_layer = {"layer": lax.rem(layer + 1, layers)}
    prev_layer = {"layer": lax.rem(layer + layers - 1, layers)}
    last = rows - 1
    sweeps = OUTER * SWEEPS
    factors = chebyshev_terms(SWEEPS)
    f32 = jnp.float32
    zero = f32(0.0)
    row_shape = (blocks, LANES)

    cells_in = pltpu.make_async_copy(cells_hbm, own_cells, via_sem.at[0])
    counts_in = pltpu.make_async_copy(counts_hbm, own_counts, via_sem.at[1])
    cells_in.start()

    def load_volts(r, _):
        pltpu.make_async_copy(
            volts_hbm.at[r // SUB, :, lax.rem(r, SUB)], x.at[0, r], in_sem.at[0]
        ).start()
        return 0

    def load_links(r, _):
        for k in range(2):
            pltpu.make_async_copy(
                class_hbm.at[k, r // SUB, :, lax.rem(r, SUB)], cls.at[k, r], class_sem.at[0]
            ).start()
        return 0

    def load_loads(r, _):
        pltpu.make_async_copy(
            loads_hbm.at[r // SUB, :, lax.rem(r, SUB)], drawn.at[r], in_sem.at[1]
        ).start()
        return 0

    barrier = pltpu.get_barrier_semaphore()
    for peer in (next_layer, prev_layer, next_tile, prev_tile):
        pl.semaphore_signal(barrier, inc=1, device_id=peer, device_id_type=MESH)

    lax.fori_loop(0, rows, load_volts, 0)
    counts_in.start()
    lax.fori_loop(0, rows, load_links, 0)
    lax.fori_loop(0, rows, load_loads, 0)

    sent = []

    def remote(src, dst, peer):
        slot = len(sent)
        copy = pltpu.make_async_remote_copy(
            src_ref=src,
            dst_ref=dst,
            send_sem=send_sem.at[slot],
            recv_sem=recv_sem.at[slot],
            device_id=peer,
            device_id_type=MESH,
        )
        copy.start()
        sent.append(copy)
        return copy

    lane = lax.broadcasted_iota(jnp.int32, row_shape, 1)
    block = lax.broadcasted_iota(jnp.int32, row_shape, 0)

    def pick(step, cells, acc, start, stop):
        def body(r, acc):
            return jnp.where(cells == r, x[step, r], acc)

        return lax.fori_loop(start, stop, body, acc, unroll=True)

    table_lane = lax.broadcasted_iota(jnp.int32, (SUB, LANES), 1)
    values = jnp.zeros((SUB, LANES), f32)
    for code in range(CLASSES):
        values = jnp.where(table_lane == code, table[0, code], values)

    def look_up(codes):
        return jnp.concatenate(
            [
                jnp.take_along_axis(
                    values, codes[SUB * k : SUB * (k + 1)], axis=1, mode="promise_in_bounds"
                )
                for k in range(blocks // SUB)
            ],
            axis=0,
        )

    cells_in.wait()
    counts_in.wait()
    pltpu.make_async_copy(x.at[1], x.at[0], in_sem.at[0]).wait()
    picked[0] = pick(0, own_cells[...], jnp.zeros(row_shape, f32), 0, rows)
    pltpu.make_async_copy(cls, cls, class_sem.at[0]).wait()
    down_links[last] = jnp.where(tile == tiles - 1, zero, look_up(cls[1, last]))

    pl.semaphore_wait(barrier, 4)
    cells_up = remote(own_cells, low_cells, next_layer)
    links_down = remote(down_links.at[last], links_in, next_tile)
    counts_up = remote(own_counts, low_counts, next_layer)
    volts_up = remote(picked.at[0], below.at[0], next_layer)

    def send_halo(outer):
        step = outer * SWEEPS
        return (
            remote(x.at[step, last], halo.at[outer, 0], next_tile),
            remote(x.at[step, 0], halo.at[outer, 1], prev_tile),
        )

    halos = send_halo(0)

    at_end = jnp.logical_and(block == blocks - 1, lane == LANES - 1)

    def look_up_row(r, _):
        links[0, r] = jnp.where(at_end, zero, look_up(cls[0, r]))

        @pl.when(r < last)
        def _():
            down_links[r] = look_up(cls[1, r])

        return 0

    lax.fori_loop(0, rows, look_up_row, 0)

    cells_up.wait_recv()
    picked[1] = pick(0, low_cells[...], jnp.zeros(row_shape, f32), 0, rows)
    volts_down = remote(picked.at[1], above.at[0], prev_layer)

    def right_of(v):
        turned = pltpu.roll(v, LANES - 1, 1)
        return jnp.where(lane == LANES - 1, pltpu.roll(turned, blocks - 1, 0), turned)

    def left_of(v):
        turned = pltpu.roll(v, 1, 1)
        return jnp.where(lane == 0, pltpu.roll(turned, 1, 0), turned)

    counts_up.wait_recv()
    pltpu.make_async_copy(drawn, drawn, in_sem.at[1]).wait()
    scale[0] = VIA_UNIT * own_counts[...].astype(f32)
    scale[1] = jnp.where(layer == 0, zero, VIA_UNIT * low_counts[...].astype(f32))
    scale[2] = jnp.zeros(row_shape, f32)
    scale[3] = jnp.zeros(row_shape, f32)

    def coefficients(r, up, down):
        own = own_cells[...] == r
        low = low_cells[...] == r
        right = links[0, r]
        left = left_of(right)
        diagonal = right + left + up + down
        diagonal = diagonal + jnp.where(own, scale[0], zero) + jnp.where(low, scale[1], zero)
        inverse = 1.0 / diagonal
        links[0, r] = inverse * right
        links[1, r] = inverse * left
        links[2, r] = inverse * up
        links[3, r] = inverse * down
        drawn[r] = inverse * drawn[r]
        scale[2] = jnp.where(own, inverse, scale[2])
        scale[3] = jnp.where(low, inverse, scale[3])

    def coefficients_row(r, _):
        coefficients(r, down_links[r - 1], down_links[r])
        return 0

    lax.fori_loop(1, rows, coefficients_row, 0)
    links_down.wait_recv()
    coefficients(0, links_in[...], down_links[0])
    scale[2] = scale[2] * scale[0]
    scale[3] = scale[3] * scale[1]
    ghosts_ready = (
        remote(links.at[:, last], ghost_links.at[0], next_tile),
        remote(links.at[:, 0], ghost_links.at[1], prev_tile),
    )

    def base_row(step, r, upper, lower):
        here = x[step, r]
        total = links[0, r] * right_of(here) + links[1, r] * left_of(here) - drawn[r]
        if upper is not None:
            total = total + links[2, r] * upper
        if lower is not None:
            total = total + links[3, r] * lower
        x[step + 1, r] = here + f32(factors[0][1]) * (total - here)

    def finish_row(step, r, flow):
        side = jnp.where(own_cells[...] == r, scale[0], zero) + jnp.where(
            low_cells[...] == r, scale[1], zero
        )
        right_side[step // SWEEPS, r] = side - drawn[r]
        if flow is not None:
            side = side + flow
        x[step + 1, r] = x[step + 1, r] + f32(factors[0][1]) * side

    def advanced(step, here, before, side, weights, upper, lower):
        fore, aft = factors[step % SWEEPS]
        total = (
            side
            + weights[0] * right_of(here)
            + weights[1] * left_of(here)
            + weights[2] * upper
            + weights[3] * lower
        )
        return here + f32(aft) * (total - here) + f32(fore) * (here - before)

    def sweep_row(step, r, upper, lower):
        weights = [links[k, r] for k in range(4)]
        x[step + 1, r] = advanced(
            step, x[step, r], x[step - 1, r], right_side[step // SWEEPS, r], weights, upper, lower
        )

    def send_out(r):
        pltpu.make_async_copy(
            x.at[sweeps, r], out_hbm.at[r // SUB, :, lax.rem(r, SUB)], out_sem
        ).start()

    for outer in range(OUTER):
        step = outer * SWEEPS
        final = outer == OUTER - 1

        def base(r, _, step=step):
            base_row(step, r, x[step, r - 1], x[step, r + 1])
            return 0

        base_row(step, 0, None, x[step, 1])
        base_row(step, last, x[step, last - 1], None)
        lax.fori_loop(1, last, base, 0)

        volts_up.wait_recv()
        volts_down.wait_recv()
        scale[0] = scale[2] * jnp.where(layer == layers - 1, f32(1.0), above[outer])
        scale[1] = scale[3] * below[outer]
        finish_row(step, 1, None)
        finish_row(step, last - 1, None)
        halos[0].wait_recv()
        finish_row(step, 0, links[2, 0] * halo[outer, 0])
        halos[1].wait_recv()
        finish_row(step, last, links[3, last] * halo[outer, 1])
        pairs = (
            remote(x.at[step + 1, pl.ds(last - 1, 2)], halo_pair.at[outer, 0], next_tile),
            remote(x.at[step + 1, pl.ds(0, 2)], halo_pair.at[outer, 1], prev_tile),
            remote(right_side.at[outer, last], halo_side.at[outer, 0], next_tile),
            remote(right_side.at[outer, 0], halo_side.at[outer, 1], prev_tile),
        )

        def finish(r, _, step=step):
            finish_row(step, r, None)
            return 0

        def second(r, _, step=step):
            sweep_row(step + 1, r, x[step + 1, r - 1], x[step + 1, r + 1])
            return 0

        def third(r, _, step=step, final=final):
            sweep_row(step + 2, r, x[step + 2, r - 1], x[step + 2, r + 1])
            if final:
                send_out(r)
            return 0

        lax.fori_loop(2, last - 1, finish, 0)
        lax.fori_loop(1, last, second, 0)
        lax.fori_loop(2, last - 1, third, 0)
        if not final:
            for k, cells in enumerate((own_cells, low_cells)):
                picked[2 * outer + 2 + k] = pick(
                    step + 3, cells[...], jnp.zeros(row_shape, f32), 2, last - 1
                )

        for copy in pairs:
            copy.wait_recv()
        if outer == 0:
            for copy in ghosts_ready:
                copy.wait_recv()
        one, two, three = step + 1, step + 2, step + 3
        upper = halo_pair[outer, 0, 1]
        lower = halo_pair[outer, 1, 0]
        ghost[0] = advanced(
            one, upper, halo[outer, 0], halo_side[outer, 0], ghost_links[0], halo_pair[outer, 0, 0], x[one, 0]
        )
        ghost[1] = advanced(
            one, lower, halo[outer, 1], halo_side[outer, 1], ghost_links[1], x[one, last], halo_pair[outer, 1, 1]
        )
        sweep_row(one, 0, upper, x[one, 1])
        sweep_row(one, last, x[one, last - 1], lower)
        sweep_row(two, 0, ghost[0], x[two, 1])
        sweep_row(two, last, x[two, last - 1], ghost[1])
        if final:
            send_out(0)
            send_out(last)
        else:
            halos = send_halo(outer + 1)
        sweep_row(two, 1, x[two, 0], x[two, 2])
        sweep_row(two, last - 1, x[two, last - 2], x[two, last])
        if final:
            send_out(1)
            send_out(last - 1)
        else:
            for k, cells in enumerate((own_cells, low_cells)):
                slot = 2 * outer + 2 + k
                acc = pick(three, cells[...], picked[slot], 0, 2)
                picked[slot] = pick(three, cells[...], acc, last - 1, rows)
                if k == 0:
                    volts_up = remote(picked.at[slot], below.at[outer + 1], next_layer)
                else:
                    volts_down = remote(picked.at[slot], above.at[outer + 1], prev_layer)

    pltpu.make_async_copy(x.at[sweeps], x.at[sweeps], out_sem).wait()
    for copy in sent:
        copy.wait_send()


def local(class_index, class_conductance, loads, start_volts, via_cells, via_counts):
    rows, cols = loads.shape[1:]
    blocks = cols // LANES
    groups = rows // SUB

    def folded(a):
        lead = a.shape[:-2]
        a = a.reshape(*lead, groups, SUB, blocks, LANES)
        return jnp.swapaxes(a, -3, -2)

    classes = folded(class_index[0])
    drawn = folded(loads[0])
    volts = folded(start_volts[0])
    cells = via_cells.reshape(blocks, LANES)
    counts = via_counts.reshape(blocks, LANES)
    grid = (rows, blocks, LANES)
    row = (blocks, LANES)
    f32, i32 = jnp.float32, jnp.int32
    copies = 5 + 2 * (OUTER - 1) + 2 * OUTER + 4 * OUTER + 2
    vmem = pltpu.VMEM


    out = pl.pallas_call(
        functools.partial(kernel, rows, blocks),
        out_shape=jax.ShapeDtypeStruct((groups, blocks, SUB, LANES), f32),
        in_specs=[pl.BlockSpec(memory_space=pltpu.SMEM)] + [pl.BlockSpec(memory_space=pl.ANY)] * 5,
        out_specs=pl.BlockSpec(memory_space=pl.ANY),
        scratch_shapes=[
            vmem((OUTER * SWEEPS + 1, *grid), f32),
            vmem((2, *grid), i32),
            vmem((4, *grid), f32),
            vmem(grid, f32),
            vmem((OUTER, *grid), f32),
            vmem(grid, f32),
            vmem(row, f32),
            vmem((2, 4, *row), f32),
            vmem((OUTER, 2, *row), f32),
            vmem((OUTER, 2, 2, *row), f32),
            vmem((OUTER, 2, *row), f32),
            vmem((2, *row), f32),
            vmem(row, i32),
            vmem(row, i32),
            vmem(row, i32),
            vmem(row, i32),
            vmem((2 * OUTER, *row), f32),
            vmem((OUTER, *row), f32),
            vmem((OUTER, *row), f32),
            vmem((4, *row), f32),
            pltpu.SemaphoreType.DMA((2,)),
            pltpu.SemaphoreType.DMA((1,)),
            pltpu.SemaphoreType.DMA((2,)),
            pltpu.SemaphoreType.DMA,
            pltpu.SemaphoreType.DMA((copies,)),
            pltpu.SemaphoreType.DMA((copies,)),
        ],
        compiler_params=pltpu.CompilerParams(
            collective_id=0, has_side_effects=True, vmem_limit_bytes=60 * 1024 * 1024
        ),
    )(class_conductance, classes, drawn, volts, cells, counts)
    return jnp.swapaxes(out, 1, 2).reshape(1, rows, cols)


def solution(mesh):
    placed = (
        P("layer", None, "tile", None),
        P("layer", None),
        P("layer", "tile", None),
        P("layer", "tile", None),
        P("layer", "tile"),
        P("layer", "tile"),
    )
    return jax.shard_map(
        local, mesh=mesh, in_specs=placed, out_specs=P("layer", "tile", None), check_vma=False
    )
```

```python
import functools

import jax
import jax.numpy as jnp
from jax import lax
from jax.experimental import pallas as pl
from jax.experimental.pallas import tpu as pltpu
from jax.sharding import PartitionSpec as P

CLASSES = 16
OUTER = 2
SWEEPS = 3
VIA_UNIT = 2.0
LOWER_BOUND = 0.05
UPPER_BOUND = 2.0
LANES = 128
SUB = 8
MESH = pl.DeviceIdType.MESH


def chebyshev_terms(count):
    centre_value = 0.5 * (UPPER_BOUND + LOWER_BOUND)
    half_width = 0.5 * (UPPER_BOUND - LOWER_BOUND)
    sigma = centre_value / half_width
    rho_last = 1.0 / sigma
    terms = [(0.0, 1.0 / centre_value)]
    for index in range(1, count):
        rho_next = 1.0 / (2.0 * sigma - rho_last)
        terms.append((rho_next * rho_last, 2.0 * rho_next / half_width))
        rho_last = rho_next
    return terms


def kernel(
    rows,
    blocks,
    table,
    class_hbm,
    loads_hbm,
    volts_hbm,
    cells_hbm,
    counts_hbm,
    out_hbm,
    x,
    cls,
    links,
    drawn,
    right_side,
    down_links,
    links_in,
    ghost_links,
    halo,
    halo_next,
    halo_part,
    part,
    own_cells,
    own_counts,
    low_cells,
    low_counts,
    picked,
    below,
    above,
    scale,
    in_sem,
    class_sem,
    via_sem,
    out_sem,
    send_sem,
    recv_sem,
):
    tile = lax.axis_index("tile")
    layer = lax.axis_index("layer")
    tiles = lax.axis_size("tile")
    layers = lax.axis_size("layer")
    next_tile = {"tile": lax.rem(tile + 1, tiles)}
    prev_tile = {"tile": lax.rem(tile + tiles - 1, tiles)}
    next_layer = {"layer": lax.rem(layer + 1, layers)}
    prev_layer = {"layer": lax.rem(layer + layers - 1, layers)}
    last = rows - 1
    sweeps = OUTER * SWEEPS
    factors = chebyshev_terms(SWEEPS)
    f32 = jnp.float32
    zero = f32(0.0)
    row_shape = (blocks, LANES)

    cells_in = pltpu.make_async_copy(cells_hbm, own_cells, via_sem.at[0])
    counts_in = pltpu.make_async_copy(counts_hbm, own_counts, via_sem.at[1])
    cells_in.start()

    def load_volts(r, _):
        pltpu.make_async_copy(
            volts_hbm.at[r // SUB, :, lax.rem(r, SUB)], x.at[0, r], in_sem.at[0]
        ).start()
        return 0

    def load_links(r, _):
        for k in range(2):
            pltpu.make_async_copy(
                class_hbm.at[k, r // SUB, :, lax.rem(r, SUB)], cls.at[k, r], class_sem.at[0]
            ).start()
        return 0

    def load_loads(r, _):
        pltpu.make_async_copy(
            loads_hbm.at[r // SUB, :, lax.rem(r, SUB)], drawn.at[r], in_sem.at[1]
        ).start()
        return 0

    barrier = pltpu.get_barrier_semaphore()
    for peer in (next_layer, prev_layer, next_tile, prev_tile):
        pl.semaphore_signal(barrier, inc=1, device_id=peer, device_id_type=MESH)

    lax.fori_loop(0, rows, load_volts, 0)
    counts_in.start()
    lax.fori_loop(0, rows, load_links, 0)
    lax.fori_loop(0, rows, load_loads, 0)

    sent = []

    def remote(src, dst, peer):
        slot = len(sent)
        copy = pltpu.make_async_remote_copy(
            src_ref=src,
            dst_ref=dst,
            send_sem=send_sem.at[slot],
            recv_sem=recv_sem.at[slot],
            device_id=peer,
            device_id_type=MESH,
        )
        copy.start()
        sent.append(copy)
        return copy

    lane = lax.broadcasted_iota(jnp.int32, row_shape, 1)
    block = lax.broadcasted_iota(jnp.int32, row_shape, 0)

    def pick(step, cells, acc, start, stop):
        def body(r, acc):
            return jnp.where(cells == r, x[step, r], acc)

        return lax.fori_loop(start, stop, body, acc, unroll=True)

    table_lane = lax.broadcasted_iota(jnp.int32, (SUB, LANES), 1)
    values = jnp.zeros((SUB, LANES), f32)
    for code in range(CLASSES):
        values = jnp.where(table_lane == code, table[0, code], values)

    def look_up(codes):
        return jnp.concatenate(
            [
                jnp.take_along_axis(
                    values, codes[SUB * k : SUB * (k + 1)], axis=1, mode="promise_in_bounds"
                )
                for k in range(blocks // SUB)
            ],
            axis=0,
        )

    cells_in.wait()
    counts_in.wait()
    pltpu.make_async_copy(x.at[1], x.at[0], in_sem.at[0]).wait()
    picked[0] = pick(0, own_cells[...], jnp.zeros(row_shape, f32), 0, rows)
    pltpu.make_async_copy(cls, cls, class_sem.at[0]).wait()
    down_links[last] = jnp.where(tile == tiles - 1, zero, look_up(cls[1, last]))

    pl.semaphore_wait(barrier, 4)
    cells_up = remote(own_cells, low_cells, next_layer)
    links_down = remote(down_links.at[last], links_in, next_tile)
    counts_up = remote(own_counts, low_counts, next_layer)
    volts_up = remote(picked.at[0], below.at[0], next_layer)

    def send_halo(outer):
        step = outer * SWEEPS
        return (
            remote(x.at[step, last], halo.at[outer, 0], next_tile),
            remote(x.at[step, 0], halo.at[outer, 1], prev_tile),
        )

    halos = send_halo(0)

    at_end = jnp.logical_and(block == blocks - 1, lane == LANES - 1)

    def look_up_row(r, _):
        links[0, r] = jnp.where(at_end, zero, look_up(cls[0, r]))

        @pl.when(r < last)
        def _():
            down_links[r] = look_up(cls[1, r])

        return 0

    lax.fori_loop(0, rows, look_up_row, 0)

    cells_up.wait_recv()
    picked[1] = pick(0, low_cells[...], jnp.zeros(row_shape, f32), 0, rows)
    volts_down = remote(picked.at[1], above.at[0], prev_layer)

    def right_of(v):
        turned = pltpu.roll(v, LANES - 1, 1)
        return jnp.where(lane == LANES - 1, pltpu.roll(turned, blocks - 1, 0), turned)

    def left_of(v):
        turned = pltpu.roll(v, 1, 1)
        return jnp.where(lane == 0, pltpu.roll(turned, 1, 0), turned)

    counts_up.wait_recv()
    pltpu.make_async_copy(drawn, drawn, in_sem.at[1]).wait()
    scale[0] = VIA_UNIT * own_counts[...].astype(f32)
    scale[1] = jnp.where(layer == 0, zero, VIA_UNIT * low_counts[...].astype(f32))
    scale[2] = jnp.zeros(row_shape, f32)
    scale[3] = jnp.zeros(row_shape, f32)

    def coefficients(r, up, down):
        own = own_cells[...] == r
        low = low_cells[...] == r
        right = links[0, r]
        left = left_of(right)
        diagonal = right + left + up + down
        diagonal = diagonal + jnp.where(own, scale[0], zero) + jnp.where(low, scale[1], zero)
        inverse = 1.0 / diagonal
        links[0, r] = inverse * right
        links[1, r] = inverse * left
        links[2, r] = inverse * up
        links[3, r] = inverse * down
        drawn[r] = inverse * drawn[r]
        scale[2] = jnp.where(own, inverse, scale[2])
        scale[3] = jnp.where(low, inverse, scale[3])

    def coefficients_row(r, _):
        coefficients(r, down_links[r - 1], down_links[r])
        return 0

    lax.fori_loop(1, rows, coefficients_row, 0)
    links_down.wait_recv()
    coefficients(0, links_in[...], down_links[0])
    scale[2] = scale[2] * scale[0]
    scale[3] = scale[3] * scale[1]
    ghosts_ready = (
        remote(links.at[3, last], ghost_links.at[0], next_tile),
        remote(links.at[2, 0], ghost_links.at[1], prev_tile),
    )

    def base_row(step, r, upper, lower):
        here = x[step, r]
        total = links[0, r] * right_of(here) + links[1, r] * left_of(here) - drawn[r]
        if upper is not None:
            total = total + links[2, r] * upper
        if lower is not None:
            total = total + links[3, r] * lower
        x[step + 1, r] = here + f32(factors[0][1]) * (total - here)

    def finish_row(step, r, flow):
        side = jnp.where(own_cells[...] == r, scale[0], zero) + jnp.where(
            low_cells[...] == r, scale[1], zero
        )
        right_side[step // SWEEPS, r] = side - drawn[r]
        if flow is not None:
            side = side + flow
        x[step + 1, r] = x[step + 1, r] + f32(factors[0][1]) * side

    def swept(step, r, upper, lower):
        fore, aft = factors[step % SWEEPS]
        here = x[step, r]
        total = (
            right_side[step // SWEEPS, r]
            + links[0, r] * right_of(here)
            + links[1, r] * left_of(here)
        )
        if upper is not None:
            total = total + links[2, r] * upper
        if lower is not None:
            total = total + links[3, r] * lower
        return here + f32(aft) * (total - here) + f32(fore) * (here - x[step - 1, r])

    def add_flow(step, value, link, other):
        return value + f32(factors[step % SWEEPS][1]) * (link * other)

    def send_out(r):
        pltpu.make_async_copy(
            x.at[sweeps, r], out_hbm.at[r // SUB, :, lax.rem(r, SUB)], out_sem
        ).start()

    for outer in range(OUTER):
        step = outer * SWEEPS
        final = outer == OUTER - 1

        def base(r, _, step=step):
            base_row(step, r, x[step, r - 1], x[step, r + 1])
            return 0

        base_row(step, 0, None, x[step, 1])
        base_row(step, last, x[step, last - 1], None)
        lax.fori_loop(1, last, base, 0)

        volts_up.wait_recv()
        volts_down.wait_recv()
        scale[0] = scale[2] * jnp.where(layer == layers - 1, f32(1.0), above[outer])
        scale[1] = scale[3] * below[outer]
        finish_row(step, 1, None)
        finish_row(step, last - 1, None)
        halos[0].wait_recv()
        finish_row(step, 0, links[2, 0] * halo[outer, 0])
        halos[1].wait_recv()
        finish_row(step, last, links[3, last] * halo[outer, 1])
        one, two, three = step + 1, step + 2, step + 3
        edges = [
            remote(x.at[one, last], halo_next.at[outer, 0], next_tile),
            remote(x.at[one, 0], halo_next.at[outer, 1], prev_tile),
        ]
        part[outer, 0] = swept(one, last, x[one, last - 1], None)
        edges.append(remote(part.at[outer, 0], halo_part.at[outer, 0], next_tile))
        part[outer, 1] = swept(one, 0, None, x[one, 1])
        edges.append(remote(part.at[outer, 1], halo_part.at[outer, 1], prev_tile))

        def finish(r, _, step=step):
            finish_row(step, r, None)
            return 0

        def second(r, _, step=step):
            x[step + 2, r] = swept(step + 1, r, x[step + 1, r - 1], x[step + 1, r + 1])
            return 0

        def third(r, _, step=step, final=final):
            x[step + 3, r] = swept(step + 2, r, x[step + 2, r - 1], x[step + 2, r + 1])
            if final:
                send_out(r)
            return 0

        lax.fori_loop(2, last - 1, finish, 0)
        lax.fori_loop(1, last, second, 0)
        lax.fori_loop(2, last - 1, third, 0)
        x[three, 1] = swept(two, 1, None, x[two, 2])
        x[three, last - 1] = swept(two, last - 1, x[two, last - 2], None)
        if not final:
            for k, cells in enumerate((own_cells, low_cells)):
                picked[2 * outer + 2 + k] = pick(
                    step + 3, cells[...], jnp.zeros(row_shape, f32), 2, last - 1
                )

        for copy in edges:
            copy.wait_recv()
        if outer == 0:
            for copy in ghosts_ready:
                copy.wait_recv()
        ghost_upper = add_flow(one, halo_part[outer, 0], ghost_links[0], x[one, 0])
        ghost_lower = add_flow(one, halo_part[outer, 1], ghost_links[1], x[one, last])
        x[two, 0] = add_flow(one, part[outer, 1], links[2, 0], halo_next[outer, 0])
        x[two, last] = add_flow(one, part[outer, 0], links[3, last], halo_next[outer, 1])
        x[three, last] = swept(two, last, x[two, last - 1], ghost_lower)
        x[three, 0] = swept(two, 0, ghost_upper, x[two, 1])
        if final:
            send_out(0)
            send_out(last)
        else:
            halos = send_halo(outer + 1)
        x[three, 1] = add_flow(two, x[three, 1], links[2, 1], x[two, 0])
        x[three, last - 1] = add_flow(two, x[three, last - 1], links[3, last - 1], x[two, last])
        if final:
            send_out(1)
            send_out(last - 1)
        else:
            for k, cells in enumerate((own_cells, low_cells)):
                slot = 2 * outer + 2 + k
                acc = pick(three, cells[...], picked[slot], 0, 2)
                picked[slot] = pick(three, cells[...], acc, last - 1, rows)
                if k == 0:
                    volts_up = remote(picked.at[slot], below.at[outer + 1], next_layer)
                else:
                    volts_down = remote(picked.at[slot], above.at[outer + 1], prev_layer)

    pltpu.make_async_copy(x.at[sweeps], x.at[sweeps], out_sem).wait()
    for copy in sent:
        copy.wait_send()


def local(class_index, class_conductance, loads, start_volts, via_cells, via_counts):
    rows, cols = loads.shape[1:]
    blocks = cols // LANES
    groups = rows // SUB

    def folded(a):
        lead = a.shape[:-2]
        a = a.reshape(*lead, groups, SUB, blocks, LANES)
        return jnp.swapaxes(a, -3, -2)

    classes = folded(class_index[0])
    drawn = folded(loads[0])
    volts = folded(start_volts[0])
    cells = via_cells.reshape(blocks, LANES)
    counts = via_counts.reshape(blocks, LANES)
    grid = (rows, blocks, LANES)
    row = (blocks, LANES)
    f32, i32 = jnp.float32, jnp.int32
    copies = 5 + 2 * (OUTER - 1) + 2 * OUTER + 4 * OUTER + 2
    vmem = pltpu.VMEM


    out = pl.pallas_call(
        functools.partial(kernel, rows, blocks),
        out_shape=pltpu.VMEM((groups, blocks, SUB, LANES), f32),
        in_specs=[pl.BlockSpec(memory_space=pltpu.SMEM)] + [pl.BlockSpec(memory_space=pl.ANY)] * 5,
        out_specs=pl.BlockSpec(memory_space=pl.ANY),
        scratch_shapes=[
            vmem((OUTER * SWEEPS + 1, *grid), f32),
            vmem((2, *grid), i32),
            vmem((4, *grid), f32),
            vmem(grid, f32),
            vmem((OUTER, *grid), f32),
            vmem(grid, f32),
            vmem(row, f32),
            vmem((2, *row), f32),
            vmem((OUTER, 2, *row), f32),
            vmem((OUTER, 2, *row), f32),
            vmem((OUTER, 2, *row), f32),
            vmem((OUTER, 2, *row), f32),
            vmem(row, i32),
            vmem(row, i32),
            vmem(row, i32),
            vmem(row, i32),
            vmem((2 * OUTER, *row), f32),
            vmem((OUTER, *row), f32),
            vmem((OUTER, *row), f32),
            vmem((4, *row), f32),
            pltpu.SemaphoreType.DMA((2,)),
            pltpu.SemaphoreType.DMA((1,)),
            pltpu.SemaphoreType.DMA((2,)),
            pltpu.SemaphoreType.DMA,
            pltpu.SemaphoreType.DMA((copies,)),
            pltpu.SemaphoreType.DMA((copies,)),
        ],
        compiler_params=pltpu.CompilerParams(
            collective_id=0, has_side_effects=True, vmem_limit_bytes=60 * 1024 * 1024
        ),
    )(class_conductance, classes, drawn, volts, cells, counts)
    return jnp.swapaxes(out, 1, 2).reshape(1, rows, cols)


def solution(mesh):
    placed = (
        P("layer", None, "tile", None),
        P("layer", None),
        P("layer", "tile", None),
        P("layer", "tile", None),
        P("layer", "tile"),
        P("layer", "tile"),
    )
    return jax.shard_map(
        local, mesh=mesh, in_specs=placed, out_specs=P("layer", "tile", None), check_vma=False
    )
```

```python
import functools

import jax
import jax.numpy as jnp
from jax import lax
from jax.experimental import pallas as pl
from jax.experimental.pallas import tpu as pltpu
from jax.sharding import PartitionSpec as P

CLASSES = 16
OUTER = 2
SWEEPS = 3
VIA_UNIT = 2.0
LOWER_BOUND = 0.05
UPPER_BOUND = 2.0
LANES = 128
SUB = 8
MESH = pl.DeviceIdType.MESH


def chebyshev_terms(count):
    centre_value = 0.5 * (UPPER_BOUND + LOWER_BOUND)
    half_width = 0.5 * (UPPER_BOUND - LOWER_BOUND)
    sigma = centre_value / half_width
    rho_last = 1.0 / sigma
    terms = [(0.0, 1.0 / centre_value)]
    for index in range(1, count):
        rho_next = 1.0 / (2.0 * sigma - rho_last)
        terms.append((rho_next * rho_last, 2.0 * rho_next / half_width))
        rho_last = rho_next
    return terms


def kernel(
    rows,
    blocks,
    table,
    class_hbm,
    loads_hbm,
    volts_hbm,
    cells_hbm,
    counts_hbm,
    out_hbm,
    x,
    cls,
    links,
    drawn,
    right_side,
    down_links,
    links_in,
    ghost_links,
    halo,
    halo_next,
    halo_part,
    part,
    own_cells,
    own_counts,
    low_cells,
    low_counts,
    picked,
    below,
    above,
    scale,
    in_sem,
    class_sem,
    via_sem,
    out_sem,
    send_sem,
    recv_sem,
):
    tile = lax.axis_index("tile")
    layer = lax.axis_index("layer")
    tiles = lax.axis_size("tile")
    layers = lax.axis_size("layer")
    next_tile = {"tile": lax.rem(tile + 1, tiles)}
    prev_tile = {"tile": lax.rem(tile + tiles - 1, tiles)}
    next_layer = {"layer": lax.rem(layer + 1, layers)}
    prev_layer = {"layer": lax.rem(layer + layers - 1, layers)}
    last = rows - 1
    sweeps = OUTER * SWEEPS
    factors = chebyshev_terms(SWEEPS)
    f32 = jnp.float32
    zero = f32(0.0)
    row_shape = (blocks, LANES)

    cells_in = pltpu.make_async_copy(cells_hbm, own_cells, via_sem.at[0])
    counts_in = pltpu.make_async_copy(counts_hbm, own_counts, via_sem.at[1])
    cells_in.start()

    def load_volts(r, _):
        pltpu.make_async_copy(
            volts_hbm.at[r // SUB, :, lax.rem(r, SUB)], x.at[0, r], in_sem.at[0]
        ).start()
        return 0

    def load_links(r, _):
        for k in range(2):
            pltpu.make_async_copy(
                class_hbm.at[k, r // SUB, :, lax.rem(r, SUB)], cls.at[k, r], class_sem.at[0]
            ).start()
        return 0

    def load_loads(r, _):
        pltpu.make_async_copy(
            loads_hbm.at[r // SUB, :, lax.rem(r, SUB)], drawn.at[r], in_sem.at[1]
        ).start()
        return 0

    barrier = pltpu.get_barrier_semaphore()
    for peer in (next_layer, prev_layer, next_tile, prev_tile):
        pl.semaphore_signal(barrier, inc=1, device_id=peer, device_id_type=MESH)

    lax.fori_loop(0, rows, load_volts, 0)
    counts_in.start()
    lax.fori_loop(0, rows, load_links, 0)
    lax.fori_loop(0, rows, load_loads, 0)

    sent = []

    def remote(src, dst, peer):
        slot = len(sent)
        copy = pltpu.make_async_remote_copy(
            src_ref=src,
            dst_ref=dst,
            send_sem=send_sem.at[slot],
            recv_sem=recv_sem.at[slot],
            device_id=peer,
            device_id_type=MESH,
        )
        copy.start()
        sent.append(copy)
        return copy

    lane = lax.broadcasted_iota(jnp.int32, row_shape, 1)
    block = lax.broadcasted_iota(jnp.int32, row_shape, 0)

    def pick(step, cells, acc, start, stop):
        def body(r, acc):
            return jnp.where(cells == r, x[step, r], acc)

        return lax.fori_loop(start, stop, body, acc, unroll=True)

    table_lane = lax.broadcasted_iota(jnp.int32, (SUB, LANES), 1)
    values = jnp.zeros((SUB, LANES), f32)
    for code in range(CLASSES):
        values = jnp.where(table_lane == code, table[0, code], values)

    def look_up(codes):
        return jnp.concatenate(
            [
                jnp.take_along_axis(
                    values, codes[SUB * k : SUB * (k + 1)], axis=1, mode="promise_in_bounds"
                )
                for k in range(blocks // SUB)
            ],
            axis=0,
        )

    cells_in.wait()
    counts_in.wait()
    pltpu.make_async_copy(x.at[1], x.at[0], in_sem.at[0]).wait()
    picked[0] = pick(0, own_cells[...], jnp.zeros(row_shape, f32), 0, rows)
    pltpu.make_async_copy(cls, cls, class_sem.at[0]).wait()
    down_links[last] = jnp.where(tile == tiles - 1, zero, look_up(cls[1, last]))

    pl.semaphore_wait(barrier, 4)
    cells_up = remote(own_cells, low_cells, next_layer)
    links_down = remote(down_links.at[last], links_in, next_tile)
    counts_up = remote(own_counts, low_counts, next_layer)
    volts_up = remote(picked.at[0], below.at[0], next_layer)

    def send_halo(outer):
        step = outer * SWEEPS
        return (
            remote(x.at[step, last], halo.at[outer, 0], next_tile),
            remote(x.at[step, 0], halo.at[outer, 1], prev_tile),
        )

    halos = send_halo(0)

    at_end = jnp.logical_and(block == blocks - 1, lane == LANES - 1)

    def look_up_row(r, _):
        links[0, r] = jnp.where(at_end, zero, look_up(cls[0, r]))
        down_links[r] = look_up(cls[1, r])
        return 0

    lax.fori_loop(0, last, look_up_row, 0, unroll=3)
    links[0, last] = jnp.where(at_end, zero, look_up(cls[0, last]))

    cells_up.wait_recv()
    picked[1] = pick(0, low_cells[...], jnp.zeros(row_shape, f32), 0, rows)
    volts_down = remote(picked.at[1], above.at[0], prev_layer)

    def right_of(v):
        turned = pltpu.roll(v, LANES - 1, 1)
        return jnp.where(lane == LANES - 1, pltpu.roll(turned, blocks - 1, 0), turned)

    def left_of(v):
        turned = pltpu.roll(v, 1, 1)
        return jnp.where(lane == 0, pltpu.roll(turned, 1, 0), turned)

    counts_up.wait_recv()
    pltpu.make_async_copy(drawn, drawn, in_sem.at[1]).wait()
    scale[0] = VIA_UNIT * own_counts[...].astype(f32)
    scale[1] = jnp.where(layer == 0, zero, VIA_UNIT * low_counts[...].astype(f32))
    scale[2] = jnp.zeros(row_shape, f32)
    scale[3] = jnp.zeros(row_shape, f32)

    def coefficients(r, up, down):
        own = own_cells[...] == r
        low = low_cells[...] == r
        right = links[0, r]
        left = left_of(right)
        diagonal = right + left + up + down
        diagonal = diagonal + jnp.where(own, scale[0], zero) + jnp.where(low, scale[1], zero)
        inverse = 1.0 / diagonal
        links[0, r] = inverse * right
        links[1, r] = inverse * left
        links[2, r] = inverse * up
        links[3, r] = inverse * down
        drawn[r] = inverse * drawn[r]
        scale[2] = jnp.where(own, inverse, scale[2])
        scale[3] = jnp.where(low, inverse, scale[3])

    def coefficients_row(r, _):
        coefficients(r, down_links[r - 1], down_links[r])
        return 0

    lax.fori_loop(1, rows, coefficients_row, 0, unroll=3)
    links_down.wait_recv()
    coefficients(0, links_in[...], down_links[0])
    scale[2] = scale[2] * scale[0]
    scale[3] = scale[3] * scale[1]
    ghosts_ready = (
        remote(links.at[3, last], ghost_links.at[0], next_tile),
        remote(links.at[2, 0], ghost_links.at[1], prev_tile),
    )

    def base_row(step, r, upper, lower):
        here = x[step, r]
        total = links[0, r] * right_of(here) + links[1, r] * left_of(here) - drawn[r]
        if upper is not None:
            total = total + links[2, r] * upper
        if lower is not None:
            total = total + links[3, r] * lower
        x[step + 1, r] = here + f32(factors[0][1]) * (total - here)

    def finish_row(step, r, flow):
        side = jnp.where(own_cells[...] == r, scale[0], zero) + jnp.where(
            low_cells[...] == r, scale[1], zero
        )
        right_side[step // SWEEPS, r] = side - drawn[r]
        if flow is not None:
            side = side + flow
        x[step + 1, r] = x[step + 1, r] + f32(factors[0][1]) * side

    def swept(step, r, upper, lower):
        fore, aft = factors[step % SWEEPS]
        here = x[step, r]
        total = (
            right_side[step // SWEEPS, r]
            + links[0, r] * right_of(here)
            + links[1, r] * left_of(here)
        )
        if upper is not None:
            total = total + links[2, r] * upper
        if lower is not None:
            total = total + links[3, r] * lower
        return here + f32(aft) * (total - here) + f32(fore) * (here - x[step - 1, r])

    def add_flow(step, value, link, other):
        return value + f32(factors[step % SWEEPS][1]) * (link * other)

    def send_out(r):
        pltpu.make_async_copy(
            x.at[sweeps, r], out_hbm.at[r // SUB, :, lax.rem(r, SUB)], out_sem
        ).start()

    for outer in range(OUTER):
        step = outer * SWEEPS
        final = outer == OUTER - 1

        def base(r, _, step=step):
            base_row(step, r, x[step, r - 1], x[step, r + 1])
            return 0

        base_row(step, 0, None, x[step, 1])
        base_row(step, last, x[step, last - 1], None)
        lax.fori_loop(1, last, base, 0, unroll=2)

        volts_up.wait_recv()
        volts_down.wait_recv()
        scale[0] = scale[2] * jnp.where(layer == layers - 1, f32(1.0), above[outer])
        scale[1] = scale[3] * below[outer]
        finish_row(step, 1, None)
        finish_row(step, last - 1, None)
        halos[0].wait_recv()
        finish_row(step, 0, links[2, 0] * halo[outer, 0])
        halos[1].wait_recv()
        finish_row(step, last, links[3, last] * halo[outer, 1])
        one, two, three = step + 1, step + 2, step + 3
        edges = [
            remote(x.at[one, last], halo_next.at[outer, 0], next_tile),
            remote(x.at[one, 0], halo_next.at[outer, 1], prev_tile),
        ]
        part[outer, 0] = swept(one, last, x[one, last - 1], None)
        edges.append(remote(part.at[outer, 0], halo_part.at[outer, 0], next_tile))
        part[outer, 1] = swept(one, 0, None, x[one, 1])
        edges.append(remote(part.at[outer, 1], halo_part.at[outer, 1], prev_tile))

        def finish(r, _, step=step):
            finish_row(step, r, None)
            return 0

        def second(r, _, step=step):
            x[step + 2, r] = swept(step + 1, r, x[step + 1, r - 1], x[step + 1, r + 1])
            return 0

        def third(r, _, step=step, final=final):
            x[step + 3, r] = swept(step + 2, r, x[step + 2, r - 1], x[step + 2, r + 1])
            if final:
                send_out(r)
            return 0

        lax.fori_loop(2, last - 1, finish, 0, unroll=2)
        lax.fori_loop(1, last, second, 0, unroll=2)
        lax.fori_loop(2, last - 1, third, 0, unroll=2)
        x[three, 1] = swept(two, 1, None, x[two, 2])
        x[three, last - 1] = swept(two, last - 1, x[two, last - 2], None)
        if not final:
            for k, cells in enumerate((own_cells, low_cells)):
                picked[2 * outer + 2 + k] = pick(
                    step + 3, cells[...], jnp.zeros(row_shape, f32), 2, last - 1
                )

        for copy in edges:
            copy.wait_recv()
        if outer == 0:
            for copy in ghosts_ready:
                copy.wait_recv()
        ghost_upper = add_flow(one, halo_part[outer, 0], ghost_links[0], x[one, 0])
        ghost_lower = add_flow(one, halo_part[outer, 1], ghost_links[1], x[one, last])
        x[two, 0] = add_flow(one, part[outer, 1], links[2, 0], halo_next[outer, 0])
        x[two, last] = add_flow(one, part[outer, 0], links[3, last], halo_next[outer, 1])
        x[three, last] = swept(two, last, x[two, last - 1], ghost_lower)
        x[three, 0] = swept(two, 0, ghost_upper, x[two, 1])
        if final:
            send_out(0)
            send_out(last)
        else:
            halos = send_halo(outer + 1)
        x[three, 1] = add_flow(two, x[three, 1], links[2, 1], x[two, 0])
        x[three, last - 1] = add_flow(two, x[three, last - 1], links[3, last - 1], x[two, last])
        if final:
            send_out(1)
            send_out(last - 1)
        else:
            for k, cells in enumerate((own_cells, low_cells)):
                slot = 2 * outer + 2 + k
                acc = pick(three, cells[...], picked[slot], 0, 2)
                picked[slot] = pick(three, cells[...], acc, last - 1, rows)
                if k == 0:
                    volts_up = remote(picked.at[slot], below.at[outer + 1], next_layer)
                else:
                    volts_down = remote(picked.at[slot], above.at[outer + 1], prev_layer)

    pltpu.make_async_copy(x.at[sweeps], x.at[sweeps], out_sem).wait()
    for copy in sent:
        copy.wait_send()


def local(class_index, class_conductance, loads, start_volts, via_cells, via_counts):
    rows, cols = loads.shape[1:]
    blocks = cols // LANES
    groups = rows // SUB

    def folded(a):
        lead = a.shape[:-2]
        a = a.reshape(*lead, groups, SUB, blocks, LANES)
        return jnp.swapaxes(a, -3, -2)

    classes = folded(class_index[0])
    drawn = folded(loads[0])
    volts = folded(start_volts[0])
    cells = via_cells.reshape(blocks, LANES)
    counts = via_counts.reshape(blocks, LANES)
    grid = (rows, blocks, LANES)
    row = (blocks, LANES)
    f32, i32 = jnp.float32, jnp.int32
    copies = 5 + 2 * (OUTER - 1) + 2 * OUTER + 4 * OUTER + 2
    vmem = pltpu.VMEM


    out = pl.pallas_call(
        functools.partial(kernel, rows, blocks),
        out_shape=pltpu.VMEM((groups, blocks, SUB, LANES), f32),
        in_specs=[pl.BlockSpec(memory_space=pltpu.SMEM)] + [pl.BlockSpec(memory_space=pl.ANY)] * 5,
        out_specs=pl.BlockSpec(memory_space=pl.ANY),
        scratch_shapes=[
            vmem((OUTER * SWEEPS + 1, *grid), f32),
            vmem((2, *grid), i32),
            vmem((4, *grid), f32),
            vmem(grid, f32),
            vmem((OUTER, *grid), f32),
            vmem(grid, f32),
            vmem(row, f32),
            vmem((2, *row), f32),
            vmem((OUTER, 2, *row), f32),
            vmem((OUTER, 2, *row), f32),
            vmem((OUTER, 2, *row), f32),
            vmem((OUTER, 2, *row), f32),
            vmem(row, i32),
            vmem(row, i32),
            vmem(row, i32),
            vmem(row, i32),
            vmem((2 * OUTER, *row), f32),
            vmem((OUTER, *row), f32),
            vmem((OUTER, *row), f32),
            vmem((4, *row), f32),
            pltpu.SemaphoreType.DMA((2,)),
            pltpu.SemaphoreType.DMA((1,)),
            pltpu.SemaphoreType.DMA((2,)),
            pltpu.SemaphoreType.DMA,
            pltpu.SemaphoreType.DMA((copies,)),
            pltpu.SemaphoreType.DMA((copies,)),
        ],
        compiler_params=pltpu.CompilerParams(
            collective_id=0, has_side_effects=True, vmem_limit_bytes=60 * 1024 * 1024
        ),
    )(class_conductance, classes, drawn, volts, cells, counts)
    return jnp.swapaxes(out, 1, 2).reshape(1, rows, cols)


def solution(mesh):
    placed = (
        P("layer", None, "tile", None),
        P("layer", None),
        P("layer", "tile", None),
        P("layer", "tile", None),
        P("layer", "tile"),
        P("layer", "tile"),
    )
    return jax.shard_map(
        local, mesh=mesh, in_specs=placed, out_specs=P("layer", "tile", None), check_vma=False
    )
```

```python
import functools

import jax
import jax.numpy as jnp
from jax import lax
from jax.experimental import pallas as pl
from jax.experimental.pallas import tpu as pltpu
from jax.sharding import PartitionSpec as P

CLASSES = 16
OUTER = 2
SWEEPS = 3
VIA_UNIT = 2.0
LOWER_BOUND = 0.05
UPPER_BOUND = 2.0
LANES = 128
SUB = 8
MESH = pl.DeviceIdType.MESH


def chebyshev_terms(count):
    centre_value = 0.5 * (UPPER_BOUND + LOWER_BOUND)
    half_width = 0.5 * (UPPER_BOUND - LOWER_BOUND)
    sigma = centre_value / half_width
    rho_last = 1.0 / sigma
    terms = [(0.0, 1.0 / centre_value)]
    for index in range(1, count):
        rho_next = 1.0 / (2.0 * sigma - rho_last)
        terms.append((rho_next * rho_last, 2.0 * rho_next / half_width))
        rho_last = rho_next
    return terms


def kernel(
    rows,
    blocks,
    table,
    class_hbm,
    loads_hbm,
    volts_hbm,
    cells_hbm,
    counts_hbm,
    out_hbm,
    x,
    cls,
    links,
    drawn,
    right_side,
    down_links,
    links_in,
    ghost_links,
    halo,
    halo_next,
    halo_part,
    part,
    own_cells,
    own_counts,
    low_cells,
    low_counts,
    picked,
    below,
    above,
    scale,
    in_sem,
    class_sem,
    via_sem,
    out_sem,
    send_sem,
    recv_sem,
):
    tile = lax.axis_index("tile")
    layer = lax.axis_index("layer")
    tiles = lax.axis_size("tile")
    layers = lax.axis_size("layer")
    next_tile = {"tile": lax.rem(tile + 1, tiles)}
    prev_tile = {"tile": lax.rem(tile + tiles - 1, tiles)}
    next_layer = {"layer": lax.rem(layer + 1, layers)}
    prev_layer = {"layer": lax.rem(layer + layers - 1, layers)}
    last = rows - 1
    sweeps = OUTER * SWEEPS
    factors = chebyshev_terms(SWEEPS)
    f32 = jnp.float32
    zero = f32(0.0)
    row_shape = (blocks, LANES)

    cells_in = pltpu.make_async_copy(cells_hbm, own_cells, via_sem.at[0])
    counts_in = pltpu.make_async_copy(counts_hbm, own_counts, via_sem.at[1])
    cells_in.start()

    def load_volts(r, _):
        pltpu.make_async_copy(
            volts_hbm.at[r // SUB, :, lax.rem(r, SUB)], x.at[0, r], in_sem.at[0]
        ).start()
        return 0

    def load_links(r, _):
        for k in range(2):
            pltpu.make_async_copy(
                class_hbm.at[k, r // SUB, :, lax.rem(r, SUB)], cls.at[k, r], class_sem.at[0]
            ).start()
        return 0

    def load_loads(r, _):
        pltpu.make_async_copy(
            loads_hbm.at[r // SUB, :, lax.rem(r, SUB)], drawn.at[r], in_sem.at[1]
        ).start()
        return 0

    barrier = pltpu.get_barrier_semaphore()
    for peer in (next_layer, prev_layer, next_tile, prev_tile):
        pl.semaphore_signal(barrier, inc=1, device_id=peer, device_id_type=MESH)

    lax.fori_loop(0, rows, load_volts, 0)
    counts_in.start()
    lax.fori_loop(0, rows, load_links, 0)
    lax.fori_loop(0, rows, load_loads, 0)

    sent = []

    def remote(src, dst, peer):
        slot = len(sent)
        copy = pltpu.make_async_remote_copy(
            src_ref=src,
            dst_ref=dst,
            send_sem=send_sem.at[slot],
            recv_sem=recv_sem.at[slot],
            device_id=peer,
            device_id_type=MESH,
        )
        copy.start()
        sent.append(copy)
        return copy

    lane = lax.broadcasted_iota(jnp.int32, row_shape, 1)
    block = lax.broadcasted_iota(jnp.int32, row_shape, 0)

    def pick(step, cells, acc, start, stop):
        def body(r, acc):
            return jnp.where(cells == r, x[step, r], acc)

        return lax.fori_loop(start, stop, body, acc, unroll=True)

    table_lane = lax.broadcasted_iota(jnp.int32, (SUB, LANES), 1)
    values = jnp.zeros((SUB, LANES), f32)
    for code in range(CLASSES):
        values = jnp.where(table_lane == code, table[0, code], values)

    def look_up(codes):
        return jnp.concatenate(
            [
                jnp.take_along_axis(
                    values, codes[SUB * k : SUB * (k + 1)], axis=1, mode="promise_in_bounds"
                )
                for k in range(blocks // SUB)
            ],
            axis=0,
        )

    cells_in.wait()
    counts_in.wait()
    pltpu.make_async_copy(x.at[1], x.at[0], in_sem.at[0]).wait()
    picked[0] = pick(0, own_cells[...], jnp.zeros(row_shape, f32), 0, rows)
    pltpu.make_async_copy(cls, cls, class_sem.at[0]).wait()
    down_links[last] = jnp.where(tile == tiles - 1, zero, look_up(cls[1, last]))

    pl.semaphore_wait(barrier, 4)
    cells_up = remote(own_cells, low_cells, next_layer)
    links_down = remote(down_links.at[last], links_in, next_tile)
    counts_up = remote(own_counts, low_counts, next_layer)
    volts_up = remote(picked.at[0], below.at[0], next_layer)

    def send_halo(outer):
        step = outer * SWEEPS
        return (
            remote(x.at[step, last], halo.at[outer, 0], next_tile),
            remote(x.at[step, 0], halo.at[outer, 1], prev_tile),
        )

    halos = send_halo(0)

    at_end = jnp.logical_and(block == blocks - 1, lane == LANES - 1)

    def look_up_row(r, _):
        links[0, r] = jnp.where(at_end, zero, look_up(cls[0, r]))
        down_links[r] = look_up(cls[1, r])
        return 0

    lax.fori_loop(0, last, look_up_row, 0, unroll=3)
    links[0, last] = jnp.where(at_end, zero, look_up(cls[0, last]))

    cells_up.wait_recv()
    picked[1] = pick(0, low_cells[...], jnp.zeros(row_shape, f32), 0, rows)
    volts_down = remote(picked.at[1], above.at[0], prev_layer)

    def right_of(v):
        turned = pltpu.roll(v, LANES - 1, 1)
        return jnp.where(lane == LANES - 1, pltpu.roll(turned, blocks - 1, 0), turned)

    def left_of(v):
        turned = pltpu.roll(v, 1, 1)
        return jnp.where(lane == 0, pltpu.roll(turned, 1, 0), turned)

    counts_up.wait_recv()
    pltpu.make_async_copy(drawn, drawn, in_sem.at[1]).wait()
    scale[0] = VIA_UNIT * own_counts[...].astype(f32)
    scale[1] = jnp.where(layer == 0, zero, VIA_UNIT * low_counts[...].astype(f32))
    scale[2] = jnp.zeros(row_shape, f32)
    scale[3] = jnp.zeros(row_shape, f32)

    def coefficients(r, up, down):
        own = own_cells[...] == r
        low = low_cells[...] == r
        right = links[0, r]
        left = left_of(right)
        diagonal = right + left + up + down
        diagonal = diagonal + jnp.where(own, scale[0], zero) + jnp.where(low, scale[1], zero)
        inverse = 1.0 / diagonal
        links[0, r] = inverse * right
        links[1, r] = inverse * left
        links[2, r] = inverse * up
        links[3, r] = inverse * down
        drawn[r] = inverse * drawn[r]
        scale[2] = jnp.where(own, inverse, scale[2])
        scale[3] = jnp.where(low, inverse, scale[3])

    def coefficients_row(r, _):
        coefficients(r, down_links[r - 1], down_links[r])
        return 0

    lax.fori_loop(1, rows, coefficients_row, 0, unroll=3)
    links_down.wait_recv()
    coefficients(0, links_in[...], down_links[0])
    scale[2] = scale[2] * scale[0]
    scale[3] = scale[3] * scale[1]
    ghosts_ready = (
        remote(links.at[3, last], ghost_links.at[0], next_tile),
        remote(links.at[2, 0], ghost_links.at[1], prev_tile),
    )

    def base_row(step, r, upper, lower):
        here = x[step, r]
        total = links[0, r] * right_of(here) + links[1, r] * left_of(here) - drawn[r]
        if upper is not None:
            total = total + links[2, r] * upper
        if lower is not None:
            total = total + links[3, r] * lower
        x[step + 1, r] = here + f32(factors[0][1]) * (total - here)

    def finish_row(step, r, flow):
        side = jnp.where(own_cells[...] == r, scale[0], zero) + jnp.where(
            low_cells[...] == r, scale[1], zero
        )
        right_side[step // SWEEPS, r] = side - drawn[r]
        if flow is not None:
            side = side + flow
        x[step + 1, r] = x[step + 1, r] + f32(factors[0][1]) * side

    def swept(step, r, upper, lower):
        fore, aft = factors[step % SWEEPS]
        here = x[step, r]
        total = (
            right_side[step // SWEEPS, r]
            + links[0, r] * right_of(here)
            + links[1, r] * left_of(here)
        )
        if upper is not None:
            total = total + links[2, r] * upper
        if lower is not None:
            total = total + links[3, r] * lower
        return here + f32(aft) * (total - here) + f32(fore) * (here - x[step - 1, r])

    def add_flow(step, value, link, other):
        return value + f32(factors[step % SWEEPS][1]) * (link * other)

    def send_out(r):
        pltpu.make_async_copy(
            x.at[sweeps, r], out_hbm.at[r // SUB, :, lax.rem(r, SUB)], out_sem
        ).start()

    for outer in range(OUTER):
        step = outer * SWEEPS
        final = outer == OUTER - 1

        def base(r, _, step=step):
            base_row(step, r, x[step, r - 1], x[step, r + 1])
            return 0

        base_row(step, 0, None, x[step, 1])
        base_row(step, last, x[step, last - 1], None)
        lax.fori_loop(1, last, base, 0, unroll=2)

        volts_up.wait_recv()
        volts_down.wait_recv()
        scale[0] = scale[2] * jnp.where(layer == layers - 1, f32(1.0), above[outer])
        scale[1] = scale[3] * below[outer]
        one, two, three = step + 1, step + 2, step + 3
        halos[0].wait_recv()
        finish_row(step, 0, links[2, 0] * halo[outer, 0])
        halos[1].wait_recv()
        finish_row(step, last, links[3, last] * halo[outer, 1])
        edges = [
            remote(x.at[one, last], halo_next.at[outer, 0], next_tile),
            remote(x.at[one, 0], halo_next.at[outer, 1], prev_tile),
        ]
        finish_row(step, 1, None)
        finish_row(step, last - 1, None)
        part[outer, 0] = swept(one, last, x[one, last - 1], None)
        edges.append(remote(part.at[outer, 0], halo_part.at[outer, 0], next_tile))
        part[outer, 1] = swept(one, 0, None, x[one, 1])
        edges.append(remote(part.at[outer, 1], halo_part.at[outer, 1], prev_tile))

        def finish(r, _, step=step):
            finish_row(step, r, None)
            return 0

        def second(r, _, step=step):
            x[step + 2, r] = swept(step + 1, r, x[step + 1, r - 1], x[step + 1, r + 1])
            return 0

        def third(r, _, step=step, final=final):
            x[step + 3, r] = swept(step + 2, r, x[step + 2, r - 1], x[step + 2, r + 1])
            if final:
                send_out(r)
            return 0

        lax.fori_loop(2, last - 1, finish, 0, unroll=2)
        lax.fori_loop(1, last, second, 0, unroll=2)
        lax.fori_loop(2, last - 1, third, 0, unroll=2)
        x[three, 1] = swept(two, 1, None, x[two, 2])
        x[three, last - 1] = swept(two, last - 1, x[two, last - 2], None)
        if not final:
            for k, cells in enumerate((own_cells, low_cells)):
                picked[2 * outer + 2 + k] = pick(
                    step + 3, cells[...], jnp.zeros(row_shape, f32), 2, last - 1
                )

        for copy in edges[:2]:
            copy.wait_recv()
        x[two, 0] = add_flow(one, part[outer, 1], links[2, 0], halo_next[outer, 0])
        x[two, last] = add_flow(one, part[outer, 0], links[3, last], halo_next[outer, 1])
        x[three, last] = swept(two, last, x[two, last - 1], None)
        x[three, 0] = swept(two, 0, None, x[two, 1])
        for r, k, edge in ((1, 2, 0), (last - 1, 3, last)):
            x[three, r] = add_flow(two, x[three, r], links[k, r], x[two, edge])
            if final:
                send_out(r)
            else:
                for slot, cells in ((2 * outer + 2, own_cells), (2 * outer + 3, low_cells)):
                    picked[slot] = jnp.where(cells[...] == r, x[three, r], picked[slot])
        if outer == 0:
            for copy in ghosts_ready:
                copy.wait_recv()
        for copy in edges[2:]:
            copy.wait_recv()
        ghost_upper = add_flow(one, halo_part[outer, 0], ghost_links[0], x[one, 0])
        ghost_lower = add_flow(one, halo_part[outer, 1], ghost_links[1], x[one, last])
        x[three, 0] = add_flow(two, x[three, 0], links[2, 0], ghost_upper)
        x[three, last] = add_flow(two, x[three, last], links[3, last], ghost_lower)
        if final:
            send_out(0)
            send_out(last)
        else:
            halos = send_halo(outer + 1)
            for slot, cells in ((2 * outer + 2, own_cells), (2 * outer + 3, low_cells)):
                acc = jnp.where(cells[...] == 0, x[three, 0], picked[slot])
                picked[slot] = jnp.where(cells[...] == last, x[three, last], acc)
            volts_up = remote(picked.at[2 * outer + 2], below.at[outer + 1], next_layer)
            volts_down = remote(picked.at[2 * outer + 3], above.at[outer + 1], prev_layer)

    pltpu.make_async_copy(x.at[sweeps], x.at[sweeps], out_sem).wait()
    for copy in sent:
        copy.wait_send()


def local(class_index, class_conductance, loads, start_volts, via_cells, via_counts):
    rows, cols = loads.shape[1:]
    blocks = cols // LANES
    groups = rows // SUB

    def folded(a):
        lead = a.shape[:-2]
        a = a.reshape(*lead, groups, SUB, blocks, LANES)
        return jnp.swapaxes(a, -3, -2)

    classes = folded(class_index[0])
    drawn = folded(loads[0])
    volts = folded(start_volts[0])
    cells = via_cells.reshape(blocks, LANES)
    counts = via_counts.reshape(blocks, LANES)
    grid = (rows, blocks, LANES)
    row = (blocks, LANES)
    f32, i32 = jnp.float32, jnp.int32
    copies = 5 + 2 * (OUTER - 1) + 2 * OUTER + 4 * OUTER + 2
    vmem = pltpu.VMEM


    out = pl.pallas_call(
        functools.partial(kernel, rows, blocks),
        out_shape=pltpu.VMEM((groups, blocks, SUB, LANES), f32),
        in_specs=[pl.BlockSpec(memory_space=pltpu.SMEM)] + [pl.BlockSpec(memory_space=pl.ANY)] * 5,
        out_specs=pl.BlockSpec(memory_space=pl.ANY),
        scratch_shapes=[
            vmem((OUTER * SWEEPS + 1, *grid), f32),
            vmem((2, *grid), i32),
            vmem((4, *grid), f32),
            vmem(grid, f32),
            vmem((OUTER, *grid), f32),
            vmem(grid, f32),
            vmem(row, f32),
            vmem((2, *row), f32),
            vmem((OUTER, 2, *row), f32),
            vmem((OUTER, 2, *row), f32),
            vmem((OUTER, 2, *row), f32),
            vmem((OUTER, 2, *row), f32),
            vmem(row, i32),
            vmem(row, i32),
            vmem(row, i32),
            vmem(row, i32),
            vmem((2 * OUTER, *row), f32),
            vmem((OUTER, *row), f32),
            vmem((OUTER, *row), f32),
            vmem((4, *row), f32),
            pltpu.SemaphoreType.DMA((2,)),
            pltpu.SemaphoreType.DMA((1,)),
            pltpu.SemaphoreType.DMA((2,)),
            pltpu.SemaphoreType.DMA,
            pltpu.SemaphoreType.DMA((copies,)),
            pltpu.SemaphoreType.DMA((copies,)),
        ],
        compiler_params=pltpu.CompilerParams(
            collective_id=0, has_side_effects=True, vmem_limit_bytes=60 * 1024 * 1024
        ),
    )(class_conductance, classes, drawn, volts, cells, counts)
    return jnp.swapaxes(out, 1, 2).reshape(1, rows, cols)


def solution(mesh):
    placed = (
        P("layer", None, "tile", None),
        P("layer", None),
        P("layer", "tile", None),
        P("layer", "tile", None),
        P("layer", "tile"),
        P("layer", "tile"),
    )
    return jax.shard_map(
        local, mesh=mesh, in_specs=placed, out_specs=P("layer", "tile", None), check_vma=False
    )
```

```python
import functools

import jax
import jax.numpy as jnp
from jax import lax
from jax.experimental import pallas as pl
from jax.experimental.pallas import tpu as pltpu
from jax.sharding import PartitionSpec as P

CLASSES = 16
OUTER = 2
SWEEPS = 3
VIA_UNIT = 2.0
LOWER_BOUND = 0.05
UPPER_BOUND = 2.0
LANES = 128
SUB = 8
MESH = pl.DeviceIdType.MESH


def chebyshev_terms(count):
    centre_value = 0.5 * (UPPER_BOUND + LOWER_BOUND)
    half_width = 0.5 * (UPPER_BOUND - LOWER_BOUND)
    sigma = centre_value / half_width
    rho_last = 1.0 / sigma
    terms = [(0.0, 1.0 / centre_value)]
    for index in range(1, count):
        rho_next = 1.0 / (2.0 * sigma - rho_last)
        terms.append((rho_next * rho_last, 2.0 * rho_next / half_width))
        rho_last = rho_next
    return terms


def when(condition, action):
    if condition is None:
        action()
    else:

        @pl.when(condition)
        def _():
            action()


class Message:
    def __init__(self, copy, sends, receives):
        self.copy, self.sends, self.receives = copy, sends, receives

    def wait_recv(self):
        when(self.receives, self.copy.wait_recv)

    def wait_send(self):
        when(self.sends, self.copy.wait_send)


def kernel(
    rows,
    blocks,
    table,
    class_hbm,
    loads_hbm,
    volts_hbm,
    cells_hbm,
    counts_hbm,
    out_hbm,
    x,
    cls,
    links,
    drawn,
    right_side,
    down_links,
    links_in,
    ghost_links,
    halo,
    halo_next,
    halo_part,
    part,
    own_cells,
    own_counts,
    low_cells,
    low_counts,
    picked,
    below,
    above,
    scale,
    in_sem,
    class_sem,
    via_sem,
    out_sem,
    send_sem,
    recv_sem,
):
    tile = lax.axis_index("tile")
    layer = lax.axis_index("layer")
    tiles = lax.axis_size("tile")
    layers = lax.axis_size("layer")
    next_tile = {"tile": lax.rem(tile + 1, tiles)}
    prev_tile = {"tile": lax.rem(tile + tiles - 1, tiles)}
    next_layer = {"layer": lax.rem(layer + 1, layers)}
    prev_layer = {"layer": lax.rem(layer + layers - 1, layers)}
    last = rows - 1
    sweeps = OUTER * SWEEPS
    factors = chebyshev_terms(SWEEPS)
    f32 = jnp.float32
    zero = f32(0.0)
    row_shape = (blocks, LANES)

    cells_in = pltpu.make_async_copy(cells_hbm, own_cells, via_sem.at[0])
    counts_in = pltpu.make_async_copy(counts_hbm, own_counts, via_sem.at[1])
    cells_in.start()

    def load_volts(r, _):
        pltpu.make_async_copy(
            volts_hbm.at[r // SUB, :, lax.rem(r, SUB)], x.at[0, r], in_sem.at[0]
        ).start()
        return 0

    def load_links(r, _):
        for k in range(2):
            pltpu.make_async_copy(
                class_hbm.at[k, r // SUB, :, lax.rem(r, SUB)], cls.at[k, r], class_sem.at[0]
            ).start()
        return 0

    def load_loads(r, _):
        pltpu.make_async_copy(
            loads_hbm.at[r // SUB, :, lax.rem(r, SUB)], drawn.at[r], in_sem.at[1]
        ).start()
        return 0

    has_prev = tile > 0
    has_next = tile < tiles - 1
    barrier = pltpu.get_barrier_semaphore()
    for peer, there in (
        (next_layer, None),
        (prev_layer, None),
        (next_tile, has_next),
        (prev_tile, has_prev),
    ):
        when(
            there,
            functools.partial(
                pl.semaphore_signal, barrier, inc=1, device_id=peer, device_id_type=MESH
            ),
        )

    lax.fori_loop(0, rows, load_volts, 0)
    counts_in.start()
    lax.fori_loop(0, rows, load_links, 0)
    lax.fori_loop(0, rows, load_loads, 0)

    sent = []

    def remote(src, dst, peer):
        slot = len(sent)
        copy = pltpu.make_async_remote_copy(
            src_ref=src,
            dst_ref=dst,
            send_sem=send_sem.at[slot],
            recv_sem=recv_sem.at[slot],
            device_id=peer,
            device_id_type=MESH,
        )
        sends, receives = None, None
        if peer is next_tile:
            sends, receives = has_next, has_prev
        elif peer is prev_tile:
            sends, receives = has_prev, has_next
        when(sends, copy.start)
        sent.append(Message(copy, sends, receives))
        return sent[-1]

    lane = lax.broadcasted_iota(jnp.int32, row_shape, 1)
    block = lax.broadcasted_iota(jnp.int32, row_shape, 0)

    def pick(step, cells, acc, start, stop):
        def body(r, acc):
            return jnp.where(cells == r, x[step, r], acc)

        return lax.fori_loop(start, stop, body, acc, unroll=True)

    table_lane = lax.broadcasted_iota(jnp.int32, (SUB, LANES), 1)
    values = jnp.zeros((SUB, LANES), f32)
    for code in range(CLASSES):
        values = jnp.where(table_lane == code, table[0, code], values)

    def look_up(codes):
        return jnp.concatenate(
            [
                jnp.take_along_axis(
                    values, codes[SUB * k : SUB * (k + 1)], axis=1, mode="promise_in_bounds"
                )
                for k in range(blocks // SUB)
            ],
            axis=0,
        )

    def no_neighbour(side):
        blank = jnp.zeros(row_shape, f32)
        ghost_links[side] = blank
        for outer in range(OUTER):
            halo[outer, side] = blank
            halo_next[outer, side] = blank
            halo_part[outer, side] = blank
        if side == 0:
            links_in[...] = blank

    when(jnp.logical_not(has_prev), lambda: no_neighbour(0))
    when(jnp.logical_not(has_next), lambda: no_neighbour(1))

    cells_in.wait()
    counts_in.wait()
    pltpu.make_async_copy(x.at[1], x.at[0], in_sem.at[0]).wait()
    picked[0] = pick(0, own_cells[...], jnp.zeros(row_shape, f32), 0, rows)
    pltpu.make_async_copy(cls, cls, class_sem.at[0]).wait()
    down_links[last] = jnp.where(tile == tiles - 1, zero, look_up(cls[1, last]))

    inside = jnp.logical_and(has_prev, has_next)
    when(inside, lambda: pl.semaphore_wait(barrier, 4))
    when(jnp.logical_not(inside), lambda: pl.semaphore_wait(barrier, 3))
    cells_up = remote(own_cells, low_cells, next_layer)
    links_down = remote(down_links.at[last], links_in, next_tile)
    counts_up = remote(own_counts, low_counts, next_layer)
    volts_up = remote(picked.at[0], below.at[0], next_layer)

    def send_halo(outer):
        step = outer * SWEEPS
        return (
            remote(x.at[step, last], halo.at[outer, 0], next_tile),
            remote(x.at[step, 0], halo.at[outer, 1], prev_tile),
        )

    halos = send_halo(0)

    at_end = jnp.logical_and(block == blocks - 1, lane == LANES - 1)

    def look_up_row(r, _):
        links[0, r] = jnp.where(at_end, zero, look_up(cls[0, r]))
        down_links[r] = look_up(cls[1, r])
        return 0

    lax.fori_loop(0, last, look_up_row, 0, unroll=3)
    links[0, last] = jnp.where(at_end, zero, look_up(cls[0, last]))

    cells_up.wait_recv()
    picked[1] = pick(0, low_cells[...], jnp.zeros(row_shape, f32), 0, rows)
    volts_down = remote(picked.at[1], above.at[0], prev_layer)

    def right_of(v):
        turned = pltpu.roll(v, LANES - 1, 1)
        return jnp.where(lane == LANES - 1, pltpu.roll(turned, blocks - 1, 0), turned)

    def left_of(v):
        turned = pltpu.roll(v, 1, 1)
        return jnp.where(lane == 0, pltpu.roll(turned, 1, 0), turned)

    counts_up.wait_recv()
    pltpu.make_async_copy(drawn, drawn, in_sem.at[1]).wait()
    scale[0] = VIA_UNIT * own_counts[...].astype(f32)
    scale[1] = jnp.where(layer == 0, zero, VIA_UNIT * low_counts[...].astype(f32))
    scale[2] = jnp.zeros(row_shape, f32)
    scale[3] = jnp.zeros(row_shape, f32)

    def coefficients(r, up, down):
        own = own_cells[...] == r
        low = low_cells[...] == r
        right = links[0, r]
        left = left_of(right)
        diagonal = right + left + up + down
        diagonal = diagonal + jnp.where(own, scale[0], zero) + jnp.where(low, scale[1], zero)
        inverse = 1.0 / diagonal
        links[0, r] = inverse * right
        links[1, r] = inverse * left
        links[2, r] = inverse * up
        links[3, r] = inverse * down
        drawn[r] = inverse * drawn[r]
        scale[2] = jnp.where(own, inverse, scale[2])
        scale[3] = jnp.where(low, inverse, scale[3])

    def coefficients_row(r, _):
        coefficients(r, down_links[r - 1], down_links[r])
        return 0

    lax.fori_loop(1, rows, coefficients_row, 0, unroll=3)
    links_down.wait_recv()
    coefficients(0, links_in[...], down_links[0])
    scale[2] = scale[2] * scale[0]
    scale[3] = scale[3] * scale[1]
    ghosts_ready = (
        remote(links.at[3, last], ghost_links.at[0], next_tile),
        remote(links.at[2, 0], ghost_links.at[1], prev_tile),
    )

    def base_row(step, r, upper, lower):
        here = x[step, r]
        total = links[0, r] * right_of(here) + links[1, r] * left_of(here) - drawn[r]
        if upper is not None:
            total = total + links[2, r] * upper
        if lower is not None:
            total = total + links[3, r] * lower
        x[step + 1, r] = here + f32(factors[0][1]) * (total - here)

    def finish_row(step, r, flow):
        side = jnp.where(own_cells[...] == r, scale[0], zero) + jnp.where(
            low_cells[...] == r, scale[1], zero
        )
        right_side[step // SWEEPS, r] = side - drawn[r]
        if flow is not None:
            side = side + flow
        x[step + 1, r] = x[step + 1, r] + f32(factors[0][1]) * side

    def swept(step, r, upper, lower):
        fore, aft = factors[step % SWEEPS]
        here = x[step, r]
        total = (
            right_side[step // SWEEPS, r]
            + links[0, r] * right_of(here)
            + links[1, r] * left_of(here)
        )
        if upper is not None:
            total = total + links[2, r] * upper
        if lower is not None:
            total = total + links[3, r] * lower
        return here + f32(aft) * (total - here) + f32(fore) * (here - x[step - 1, r])

    def add_flow(step, value, link, other):
        return value + f32(factors[step % SWEEPS][1]) * (link * other)

    def send_out(r):
        pltpu.make_async_copy(
            x.at[sweeps, r], out_hbm.at[r // SUB, :, lax.rem(r, SUB)], out_sem
        ).start()

    for outer in range(OUTER):
        step = outer * SWEEPS
        final = outer == OUTER - 1

        def base(r, _, step=step):
            base_row(step, r, x[step, r - 1], x[step, r + 1])
            return 0

        base_row(step, 0, None, x[step, 1])
        base_row(step, last, x[step, last - 1], None)
        lax.fori_loop(1, last, base, 0, unroll=2)

        volts_up.wait_recv()
        volts_down.wait_recv()
        scale[0] = scale[2] * jnp.where(layer == layers - 1, f32(1.0), above[outer])
        scale[1] = scale[3] * below[outer]
        one, two, three = step + 1, step + 2, step + 3
        halos[0].wait_recv()
        finish_row(step, 0, links[2, 0] * halo[outer, 0])
        halos[1].wait_recv()
        finish_row(step, last, links[3, last] * halo[outer, 1])
        edges = [
            remote(x.at[one, last], halo_next.at[outer, 0], next_tile),
            remote(x.at[one, 0], halo_next.at[outer, 1], prev_tile),
        ]
        finish_row(step, 1, None)
        finish_row(step, last - 1, None)
        part[outer, 0] = swept(one, last, x[one, last - 1], None)
        edges.append(remote(part.at[outer, 0], halo_part.at[outer, 0], next_tile))
        part[outer, 1] = swept(one, 0, None, x[one, 1])
        edges.append(remote(part.at[outer, 1], halo_part.at[outer, 1], prev_tile))

        def finish(r, _, step=step):
            finish_row(step, r, None)
            return 0

        def second(r, _, step=step):
            x[step + 2, r] = swept(step + 1, r, x[step + 1, r - 1], x[step + 1, r + 1])
            return 0

        def third(r, _, step=step, final=final):
            x[step + 3, r] = swept(step + 2, r, x[step + 2, r - 1], x[step + 2, r + 1])
            if final:
                send_out(r)
            return 0

        lax.fori_loop(2, last - 1, finish, 0, unroll=2)
        lax.fori_loop(1, last, second, 0, unroll=2)
        lax.fori_loop(2, last - 1, third, 0, unroll=2)
        x[three, 1] = swept(two, 1, None, x[two, 2])
        x[three, last - 1] = swept(two, last - 1, x[two, last - 2], None)
        if not final:
            for k, cells in enumerate((own_cells, low_cells)):
                picked[2 * outer + 2 + k] = pick(
                    step + 3, cells[...], jnp.zeros(row_shape, f32), 2, last - 1
                )

        for copy in edges[:2]:
            copy.wait_recv()
        x[two, 0] = add_flow(one, part[outer, 1], links[2, 0], halo_next[outer, 0])
        x[two, last] = add_flow(one, part[outer, 0], links[3, last], halo_next[outer, 1])
        x[three, last] = swept(two, last, x[two, last - 1], None)
        x[three, 0] = swept(two, 0, None, x[two, 1])
        for r, k, edge in ((1, 2, 0), (last - 1, 3, last)):
            x[three, r] = add_flow(two, x[three, r], links[k, r], x[two, edge])
            if final:
                send_out(r)
            else:
                for slot, cells in ((2 * outer + 2, own_cells), (2 * outer + 3, low_cells)):
                    picked[slot] = jnp.where(cells[...] == r, x[three, r], picked[slot])
        if outer == 0:
            for copy in ghosts_ready:
                copy.wait_recv()
        for copy in edges[2:]:
            copy.wait_recv()
        ghost_upper = add_flow(one, halo_part[outer, 0], ghost_links[0], x[one, 0])
        ghost_lower = add_flow(one, halo_part[outer, 1], ghost_links[1], x[one, last])
        x[three, 0] = add_flow(two, x[three, 0], links[2, 0], ghost_upper)
        x[three, last] = add_flow(two, x[three, last], links[3, last], ghost_lower)
        if final:
            send_out(0)
            send_out(last)
        else:
            halos = send_halo(outer + 1)
            for slot, cells in ((2 * outer + 2, own_cells), (2 * outer + 3, low_cells)):
                acc = jnp.where(cells[...] == 0, x[three, 0], picked[slot])
                picked[slot] = jnp.where(cells[...] == last, x[three, last], acc)
            volts_up = remote(picked.at[2 * outer + 2], below.at[outer + 1], next_layer)
            volts_down = remote(picked.at[2 * outer + 3], above.at[outer + 1], prev_layer)

    pltpu.make_async_copy(x.at[sweeps], x.at[sweeps], out_sem).wait()
    for copy in sent:
        copy.wait_send()


def local(class_index, class_conductance, loads, start_volts, via_cells, via_counts):
    rows, cols = loads.shape[1:]
    blocks = cols // LANES
    groups = rows // SUB

    def folded(a):
        lead = a.shape[:-2]
        a = a.reshape(*lead, groups, SUB, blocks, LANES)
        return jnp.swapaxes(a, -3, -2)

    classes = folded(class_index[0])
    drawn = folded(loads[0])
    volts = folded(start_volts[0])
    cells = via_cells.reshape(blocks, LANES)
    counts = via_counts.reshape(blocks, LANES)
    grid = (rows, blocks, LANES)
    row = (blocks, LANES)
    f32, i32 = jnp.float32, jnp.int32
    copies = 5 + 2 * (OUTER - 1) + 2 * OUTER + 4 * OUTER + 2
    vmem = pltpu.VMEM


    out = pl.pallas_call(
        functools.partial(kernel, rows, blocks),
        out_shape=pltpu.VMEM((groups, blocks, SUB, LANES), f32),
        in_specs=[pl.BlockSpec(memory_space=pltpu.SMEM)] + [pl.BlockSpec(memory_space=pl.ANY)] * 5,
        out_specs=pl.BlockSpec(memory_space=pl.ANY),
        scratch_shapes=[
            vmem((OUTER * SWEEPS + 1, *grid), f32),
            vmem((2, *grid), i32),
            vmem((4, *grid), f32),
            vmem(grid, f32),
            vmem((OUTER, *grid), f32),
            vmem(grid, f32),
            vmem(row, f32),
            vmem((2, *row), f32),
            vmem((OUTER, 2, *row), f32),
            vmem((OUTER, 2, *row), f32),
            vmem((OUTER, 2, *row), f32),
            vmem((OUTER, 2, *row), f32),
            vmem(row, i32),
            vmem(row, i32),
            vmem(row, i32),
            vmem(row, i32),
            vmem((2 * OUTER, *row), f32),
            vmem((OUTER, *row), f32),
            vmem((OUTER, *row), f32),
            vmem((4, *row), f32),
            pltpu.SemaphoreType.DMA((2,)),
            pltpu.SemaphoreType.DMA((1,)),
            pltpu.SemaphoreType.DMA((2,)),
            pltpu.SemaphoreType.DMA,
            pltpu.SemaphoreType.DMA((copies,)),
            pltpu.SemaphoreType.DMA((copies,)),
        ],
        compiler_params=pltpu.CompilerParams(
            collective_id=0, has_side_effects=True, vmem_limit_bytes=60 * 1024 * 1024
        ),
    )(class_conductance, classes, drawn, volts, cells, counts)
    return jnp.swapaxes(out, 1, 2).reshape(1, rows, cols)


def solution(mesh):
    placed = (
        P("layer", None, "tile", None),
        P("layer", None),
        P("layer", "tile", None),
        P("layer", "tile", None),
        P("layer", "tile"),
        P("layer", "tile"),
    )
    return jax.shard_map(
        local, mesh=mesh, in_specs=placed, out_specs=P("layer", "tile", None), check_vma=False
    )
```

```python
import functools

import jax
import jax.numpy as jnp
from jax import lax
from jax.experimental import pallas as pl
from jax.experimental.pallas import tpu as pltpu
from jax.sharding import PartitionSpec as P

CLASSES = 16
OUTER = 2
SWEEPS = 3
VIA_UNIT = 2.0
LOWER_BOUND = 0.05
UPPER_BOUND = 2.0
LANES = 128
SUB = 8
MESH = pl.DeviceIdType.MESH


def chebyshev_terms(count):
    centre_value = 0.5 * (UPPER_BOUND + LOWER_BOUND)
    half_width = 0.5 * (UPPER_BOUND - LOWER_BOUND)
    sigma = centre_value / half_width
    rho_last = 1.0 / sigma
    terms = [(0.0, 1.0 / centre_value)]
    for index in range(1, count):
        rho_next = 1.0 / (2.0 * sigma - rho_last)
        terms.append((rho_next * rho_last, 2.0 * rho_next / half_width))
        rho_last = rho_next
    return terms


def when(condition, action):
    if condition is None:
        action()
    else:

        @pl.when(condition)
        def _():
            action()


class Message:
    def __init__(self, copy, sends, receives):
        self.copy, self.sends, self.receives = copy, sends, receives

    def wait_recv(self):
        when(self.receives, self.copy.wait_recv)

    def wait_send(self):
        when(self.sends, self.copy.wait_send)


def kernel(
    rows,
    blocks,
    table,
    class_hbm,
    loads_hbm,
    volts_hbm,
    cells_hbm,
    counts_hbm,
    out_hbm,
    x,
    cls,
    links,
    drawn,
    right_side,
    down_links,
    links_in,
    ghost_links,
    halo,
    halo_next,
    halo_part,
    part,
    own_cells,
    own_counts,
    low_cells,
    low_counts,
    picked,
    below,
    above,
    scale,
    in_sem,
    class_sem,
    via_sem,
    out_sem,
    send_sem,
    recv_sem,
):
    tile = lax.axis_index("tile")
    layer = lax.axis_index("layer")
    tiles = lax.axis_size("tile")
    layers = lax.axis_size("layer")
    next_tile = {"tile": lax.rem(tile + 1, tiles)}
    prev_tile = {"tile": lax.rem(tile + tiles - 1, tiles)}
    next_layer = {"layer": lax.rem(layer + 1, layers)}
    prev_layer = {"layer": lax.rem(layer + layers - 1, layers)}
    last = rows - 1
    sweeps = OUTER * SWEEPS
    factors = chebyshev_terms(SWEEPS)
    f32 = jnp.float32
    zero = f32(0.0)
    row_shape = (blocks, LANES)

    cells_in = pltpu.make_async_copy(cells_hbm, own_cells, via_sem.at[0])
    counts_in = pltpu.make_async_copy(counts_hbm, own_counts, via_sem.at[1])
    cells_in.start()

    def load_volts(r, _):
        pltpu.make_async_copy(
            volts_hbm.at[r // SUB, :, lax.rem(r, SUB)], x.at[0, r], in_sem.at[0]
        ).start()
        return 0

    def load_links(r, _):
        for k in range(2):
            pltpu.make_async_copy(
                class_hbm.at[k, r // SUB, :, lax.rem(r, SUB)], cls.at[k, r], class_sem.at[0]
            ).start()
        return 0

    def load_loads(r, _):
        pltpu.make_async_copy(
            loads_hbm.at[r // SUB, :, lax.rem(r, SUB)], drawn.at[r], in_sem.at[1]
        ).start()
        return 0

    has_lower = layer > 0
    has_upper = layer < layers - 1
    has_prev = tile > 0
    has_next = tile < tiles - 1
    barrier = pltpu.get_barrier_semaphore()
    for peer, there in (
        (next_layer, has_upper),
        (prev_layer, has_lower),
        (next_tile, has_next),
        (prev_tile, has_prev),
    ):
        when(
            there,
            functools.partial(
                pl.semaphore_signal, barrier, inc=1, device_id=peer, device_id_type=MESH
            ),
        )

    lax.fori_loop(0, rows, load_volts, 0)
    counts_in.start()
    lax.fori_loop(0, rows, load_links, 0)
    lax.fori_loop(0, rows, load_loads, 0)

    sent = []

    def remote(src, dst, peer):
        slot = len(sent)
        copy = pltpu.make_async_remote_copy(
            src_ref=src,
            dst_ref=dst,
            send_sem=send_sem.at[slot],
            recv_sem=recv_sem.at[slot],
            device_id=peer,
            device_id_type=MESH,
        )
        sends, receives = None, None
        if peer is next_tile:
            sends, receives = has_next, has_prev
        elif peer is prev_tile:
            sends, receives = has_prev, has_next
        elif peer is next_layer:
            sends, receives = has_upper, has_lower
        elif peer is prev_layer:
            sends, receives = has_lower, has_upper
        when(sends, copy.start)
        sent.append(Message(copy, sends, receives))
        return sent[-1]

    lane = lax.broadcasted_iota(jnp.int32, row_shape, 1)
    block = lax.broadcasted_iota(jnp.int32, row_shape, 0)

    def pick(step, cells, acc, start, stop):
        def body(r, acc):
            return jnp.where(cells == r, x[step, r], acc)

        return lax.fori_loop(start, stop, body, acc, unroll=True)

    table_lane = lax.broadcasted_iota(jnp.int32, (SUB, LANES), 1)
    values = jnp.zeros((SUB, LANES), f32)
    for code in range(CLASSES):
        values = jnp.where(table_lane == code, table[0, code], values)

    def look_up(codes):
        return jnp.concatenate(
            [
                jnp.take_along_axis(
                    values, codes[SUB * k : SUB * (k + 1)], axis=1, mode="promise_in_bounds"
                )
                for k in range(blocks // SUB)
            ],
            axis=0,
        )

    def no_neighbour(side):
        blank = jnp.zeros(row_shape, f32)
        ghost_links[side] = blank
        for outer in range(OUTER):
            halo[outer, side] = blank
            halo_next[outer, side] = blank
            halo_part[outer, side] = blank
        if side == 0:
            links_in[...] = blank

    def no_lower():
        low_cells[...] = jnp.zeros(row_shape, jnp.int32)
        low_counts[...] = jnp.zeros(row_shape, jnp.int32)
        for outer in range(OUTER):
            below[outer] = jnp.zeros(row_shape, f32)

    def no_upper():
        for outer in range(OUTER):
            above[outer] = jnp.zeros(row_shape, f32)

    when(jnp.logical_not(has_lower), no_lower)
    when(jnp.logical_not(has_upper), no_upper)
    when(jnp.logical_not(has_prev), lambda: no_neighbour(0))
    when(jnp.logical_not(has_next), lambda: no_neighbour(1))

    cells_in.wait()
    counts_in.wait()
    pltpu.make_async_copy(x.at[1], x.at[0], in_sem.at[0]).wait()
    picked[0] = pick(0, own_cells[...], jnp.zeros(row_shape, f32), 0, rows)
    pltpu.make_async_copy(cls, cls, class_sem.at[0]).wait()
    down_links[last] = jnp.where(tile == tiles - 1, zero, look_up(cls[1, last]))

    in_strips = jnp.logical_and(has_prev, has_next)
    in_layers = jnp.logical_and(has_lower, has_upper)
    for strips, strip_peers in ((in_strips, 2), (jnp.logical_not(in_strips), 1)):
        for inner, layer_peers in ((in_layers, 2), (jnp.logical_not(in_layers), 1)):
            when(
                jnp.logical_and(strips, inner),
                functools.partial(pl.semaphore_wait, barrier, strip_peers + layer_peers),
            )
    cells_up = remote(own_cells, low_cells, next_layer)
    links_down = remote(down_links.at[last], links_in, next_tile)
    counts_up = remote(own_counts, low_counts, next_layer)
    volts_up = remote(picked.at[0], below.at[0], next_layer)

    def send_halo(outer):
        step = outer * SWEEPS
        return (
            remote(x.at[step, last], halo.at[outer, 0], next_tile),
            remote(x.at[step, 0], halo.at[outer, 1], prev_tile),
        )

    halos = send_halo(0)

    at_end = jnp.logical_and(block == blocks - 1, lane == LANES - 1)

    def look_up_row(r, _):
        links[0, r] = jnp.where(at_end, zero, look_up(cls[0, r]))
        down_links[r] = look_up(cls[1, r])
        return 0

    lax.fori_loop(0, last, look_up_row, 0, unroll=3)
    links[0, last] = jnp.where(at_end, zero, look_up(cls[0, last]))

    cells_up.wait_recv()
    picked[1] = pick(0, low_cells[...], jnp.zeros(row_shape, f32), 0, rows)
    volts_down = remote(picked.at[1], above.at[0], prev_layer)

    def right_of(v):
        turned = pltpu.roll(v, LANES - 1, 1)
        return jnp.where(lane == LANES - 1, pltpu.roll(turned, blocks - 1, 0), turned)

    def left_of(v):
        turned = pltpu.roll(v, 1, 1)
        return jnp.where(lane == 0, pltpu.roll(turned, 1, 0), turned)

    counts_up.wait_recv()
    pltpu.make_async_copy(drawn, drawn, in_sem.at[1]).wait()
    scale[0] = VIA_UNIT * own_counts[...].astype(f32)
    scale[1] = jnp.where(layer == 0, zero, VIA_UNIT * low_counts[...].astype(f32))
    scale[2] = jnp.zeros(row_shape, f32)
    scale[3] = jnp.zeros(row_shape, f32)

    def coefficients(r, up, down):
        own = own_cells[...] == r
        low = low_cells[...] == r
        right = links[0, r]
        left = left_of(right)
        diagonal = right + left + up + down
        diagonal = diagonal + jnp.where(own, scale[0], zero) + jnp.where(low, scale[1], zero)
        inverse = 1.0 / diagonal
        links[0, r] = inverse * right
        links[1, r] = inverse * left
        links[2, r] = inverse * up
        links[3, r] = inverse * down
        drawn[r] = inverse * drawn[r]
        scale[2] = jnp.where(own, inverse, scale[2])
        scale[3] = jnp.where(low, inverse, scale[3])

    def coefficients_row(r, _):
        coefficients(r, down_links[r - 1], down_links[r])
        return 0

    lax.fori_loop(1, rows, coefficients_row, 0, unroll=3)
    links_down.wait_recv()
    coefficients(0, links_in[...], down_links[0])
    scale[2] = scale[2] * scale[0]
    scale[3] = scale[3] * scale[1]
    ghosts_ready = (
        remote(links.at[3, last], ghost_links.at[0], next_tile),
        remote(links.at[2, 0], ghost_links.at[1], prev_tile),
    )

    def base_row(step, r, upper, lower):
        here = x[step, r]
        total = links[0, r] * right_of(here) + links[1, r] * left_of(here) - drawn[r]
        if upper is not None:
            total = total + links[2, r] * upper
        if lower is not None:
            total = total + links[3, r] * lower
        x[step + 1, r] = here + f32(factors[0][1]) * (total - here)

    def finish_row(step, r, flow):
        side = jnp.where(own_cells[...] == r, scale[0], zero) + jnp.where(
            low_cells[...] == r, scale[1], zero
        )
        right_side[step // SWEEPS, r] = side - drawn[r]
        if flow is not None:
            side = side + flow
        x[step + 1, r] = x[step + 1, r] + f32(factors[0][1]) * side

    def swept(step, r, upper, lower):
        fore, aft = factors[step % SWEEPS]
        here = x[step, r]
        total = (
            right_side[step // SWEEPS, r]
            + links[0, r] * right_of(here)
            + links[1, r] * left_of(here)
        )
        if upper is not None:
            total = total + links[2, r] * upper
        if lower is not None:
            total = total + links[3, r] * lower
        return here + f32(aft) * (total - here) + f32(fore) * (here - x[step - 1, r])

    def add_flow(step, value, link, other):
        return value + f32(factors[step % SWEEPS][1]) * (link * other)

    def send_out(r):
        pltpu.make_async_copy(
            x.at[sweeps, r], out_hbm.at[r // SUB, :, lax.rem(r, SUB)], out_sem
        ).start()

    for outer in range(OUTER):
        step = outer * SWEEPS
        final = outer == OUTER - 1

        def base(r, _, step=step):
            base_row(step, r, x[step, r - 1], x[step, r + 1])
            return 0

        base_row(step, 0, None, x[step, 1])
        base_row(step, last, x[step, last - 1], None)
        lax.fori_loop(1, last, base, 0, unroll=2)

        volts_up.wait_recv()
        volts_down.wait_recv()
        scale[0] = scale[2] * jnp.where(layer == layers - 1, f32(1.0), above[outer])
        scale[1] = scale[3] * below[outer]
        one, two, three = step + 1, step + 2, step + 3
        halos[0].wait_recv()
        finish_row(step, 0, links[2, 0] * halo[outer, 0])
        halos[1].wait_recv()
        finish_row(step, last, links[3, last] * halo[outer, 1])
        edges = [
            remote(x.at[one, last], halo_next.at[outer, 0], next_tile),
            remote(x.at[one, 0], halo_next.at[outer, 1], prev_tile),
        ]
        finish_row(step, 1, None)
        finish_row(step, last - 1, None)
        part[outer, 0] = swept(one, last, x[one, last - 1], None)
        edges.append(remote(part.at[outer, 0], halo_part.at[outer, 0], next_tile))
        part[outer, 1] = swept(one, 0, None, x[one, 1])
        edges.append(remote(part.at[outer, 1], halo_part.at[outer, 1], prev_tile))

        def finish(r, _, step=step):
            finish_row(step, r, None)
            return 0

        def second(r, _, step=step):
            x[step + 2, r] = swept(step + 1, r, x[step + 1, r - 1], x[step + 1, r + 1])
            return 0

        def third(r, _, step=step, final=final):
            x[step + 3, r] = swept(step + 2, r, x[step + 2, r - 1], x[step + 2, r + 1])
            if final:
                send_out(r)
            return 0

        lax.fori_loop(2, last - 1, finish, 0, unroll=2)
        lax.fori_loop(1, last, second, 0, unroll=2)
        lax.fori_loop(2, last - 1, third, 0, unroll=2)
        x[three, 1] = swept(two, 1, None, x[two, 2])
        x[three, last - 1] = swept(two, last - 1, x[two, last - 2], None)
        if not final:
            for k, cells in enumerate((own_cells, low_cells)):
                picked[2 * outer + 2 + k] = pick(
                    step + 3, cells[...], jnp.zeros(row_shape, f32), 2, last - 1
                )

        for copy in edges[:2]:
            copy.wait_recv()
        x[two, 0] = add_flow(one, part[outer, 1], links[2, 0], halo_next[outer, 0])
        x[two, last] = add_flow(one, part[outer, 0], links[3, last], halo_next[outer, 1])
        x[three, last] = swept(two, last, x[two, last - 1], None)
        x[three, 0] = swept(two, 0, None, x[two, 1])
        for r, k, edge in ((1, 2, 0), (last - 1, 3, last)):
            x[three, r] = add_flow(two, x[three, r], links[k, r], x[two, edge])
            if final:
                send_out(r)
            else:
                for slot, cells in ((2 * outer + 2, own_cells), (2 * outer + 3, low_cells)):
                    picked[slot] = jnp.where(cells[...] == r, x[three, r], picked[slot])
        if outer == 0:
            for copy in ghosts_ready:
                copy.wait_recv()
        for copy in edges[2:]:
            copy.wait_recv()
        ghost_upper = add_flow(one, halo_part[outer, 0], ghost_links[0], x[one, 0])
        ghost_lower = add_flow(one, halo_part[outer, 1], ghost_links[1], x[one, last])
        x[three, 0] = add_flow(two, x[three, 0], links[2, 0], ghost_upper)
        x[three, last] = add_flow(two, x[three, last], links[3, last], ghost_lower)
        if final:
            send_out(0)
            send_out(last)
        else:
            halos = send_halo(outer + 1)
            for slot, cells in ((2 * outer + 2, own_cells), (2 * outer + 3, low_cells)):
                acc = jnp.where(cells[...] == 0, x[three, 0], picked[slot])
                picked[slot] = jnp.where(cells[...] == last, x[three, last], acc)
            volts_up = remote(picked.at[2 * outer + 2], below.at[outer + 1], next_layer)
            volts_down = remote(picked.at[2 * outer + 3], above.at[outer + 1], prev_layer)

    pltpu.make_async_copy(x.at[sweeps], x.at[sweeps], out_sem).wait()
    for copy in sent:
        copy.wait_send()


def local(class_index, class_conductance, loads, start_volts, via_cells, via_counts):
    rows, cols = loads.shape[1:]
    blocks = cols // LANES
    groups = rows // SUB

    def folded(a):
        lead = a.shape[:-2]
        a = a.reshape(*lead, groups, SUB, blocks, LANES)
        return jnp.swapaxes(a, -3, -2)

    classes = folded(class_index[0])
    drawn = folded(loads[0])
    volts = folded(start_volts[0])
    cells = via_cells.reshape(blocks, LANES)
    counts = via_counts.reshape(blocks, LANES)
    grid = (rows, blocks, LANES)
    row = (blocks, LANES)
    f32, i32 = jnp.float32, jnp.int32
    copies = 5 + 2 * (OUTER - 1) + 2 * OUTER + 4 * OUTER + 2
    vmem = pltpu.VMEM


    out = pl.pallas_call(
        functools.partial(kernel, rows, blocks),
        out_shape=pltpu.VMEM((groups, blocks, SUB, LANES), f32),
        in_specs=[pl.BlockSpec(memory_space=pltpu.SMEM)] + [pl.BlockSpec(memory_space=pl.ANY)] * 5,
        out_specs=pl.BlockSpec(memory_space=pl.ANY),
        scratch_shapes=[
            vmem((OUTER * SWEEPS + 1, *grid), f32),
            vmem((2, *grid), i32),
            vmem((4, *grid), f32),
            vmem(grid, f32),
            vmem((OUTER, *grid), f32),
            vmem(grid, f32),
            vmem(row, f32),
            vmem((2, *row), f32),
            vmem((OUTER, 2, *row), f32),
            vmem((OUTER, 2, *row), f32),
            vmem((OUTER, 2, *row), f32),
            vmem((OUTER, 2, *row), f32),
            vmem(row, i32),
            vmem(row, i32),
            vmem(row, i32),
            vmem(row, i32),
            vmem((2 * OUTER, *row), f32),
            vmem((OUTER, *row), f32),
            vmem((OUTER, *row), f32),
            vmem((4, *row), f32),
            pltpu.SemaphoreType.DMA((2,)),
            pltpu.SemaphoreType.DMA((1,)),
            pltpu.SemaphoreType.DMA((2,)),
            pltpu.SemaphoreType.DMA,
            pltpu.SemaphoreType.DMA((copies,)),
            pltpu.SemaphoreType.DMA((copies,)),
        ],
        compiler_params=pltpu.CompilerParams(
            collective_id=0, has_side_effects=True, vmem_limit_bytes=60 * 1024 * 1024
        ),
    )(class_conductance, classes, drawn, volts, cells, counts)
    return jnp.swapaxes(out, 1, 2).reshape(1, rows, cols)


def solution(mesh):
    placed = (
        P("layer", None, "tile", None),
        P("layer", None),
        P("layer", "tile", None),
        P("layer", "tile", None),
        P("layer", "tile"),
        P("layer", "tile"),
    )
    return jax.shard_map(
        local, mesh=mesh, in_specs=placed, out_specs=P("layer", "tile", None), check_vma=False
    )
```
